32 devices in a mesh: groups: 2 (over x), bricks: 16 (over z, y, core).
Axes of the slice: x: 2, y: 2, z: 4, core: 2. Of those that a mesh axis runs over, the one named last changes fastest.
Arguments:
- snapshots: bfloat16 [512, 32, 32, 256], P(('groups', 'bricks')), parts along dimension 0, may hold values from -30 to 30
- material: int32 [512, 1024], P(('groups', 'bricks')), parts along dimension 0, may hold values from 0 to 15
- occupancy: int32 [32, 4], P(('groups', 'bricks')), parts along dimension 0, may hold values 0 or 1
- moduli: bfloat16 [16], replicated, may hold values from 0.19921875 to 5
Outputs:
- energy_gram: float32 [512, 256], P(('groups', 'bricks')), parts along dimension 0
The draws below stay inside these ranges and needn't reach their ends.
There are 2 independent parts, one for each index of `groups`. The reference program is written for one: setup_inputs(seed, part) draws one part's arguments, and reference() takes and returns one part's arrays. A program takes and returns all parts, laid end to end along the dimension named above; an argument that names none is the same for every part. Nothing has to cross between parts.
All inputs are finite; a program needn't handle non-finite values. No bound on the sum of `occupancy` on one device may be relied on, other than what follows from the above.
Results may differ from the reference program's by a relative error of at most 0.0003.
Values may be sent and summed in bfloat16 or wider, within the bound.
No kernel may reach another device: no remote copies, remote signals or barrier semaphores. Data moves between devices by JAX's collectives and lax.ppermute only.
A program may use at most 128 MiB of HBM per device.

```python
import math
import jax
import jax.numpy as jnp
from jax import lax

S = 256
ZC = 16
GY = 32
GX = 32
CLASSES = 16
TILES = 4
Z = 256
VOXELS = 262144
N_BRICKS = 16


def draw_rates(sub_key, rate_shape, low_rate, high_rate):
    key_mag, key_sign = jax.random.split(sub_key)
    magnitude = jax.random.uniform(key_mag, rate_shape, jnp.float32, low_rate, high_rate)
    sign_values = jnp.where(jax.random.bernoulli(key_sign, 0.5, rate_shape), 1.0, -1.0)
    return magnitude * sign_values


def draw_snapshots(key, part):
    subkeys = jax.random.split(jax.random.fold_in(key, 7), 10)
    along_z = jnp.arange(Z, dtype=jnp.float32)[:, None, None, None]
    along_y = jnp.arange(GY, dtype=jnp.float32)[None, :, None, None]
    along_x = jnp.arange(GX, dtype=jnp.float32)[None, None, :, None]
    mode_z = draw_rates(subkeys[0], (3, S), 0.03, 0.3)
    mode_y = draw_rates(subkeys[1], (3, S), 0.05, 0.4)
    mode_x = draw_rates(subkeys[2], (3, S), 0.05, 0.4)
    phases = jax.random.uniform(subkeys[3], (3, S), jnp.float32, -math.pi, math.pi)
    shared_rates = draw_rates(subkeys[4], (3,), 0.03, 0.3)
    shared_phase = jax.random.uniform(subkeys[5], (), jnp.float32, -math.pi, math.pi)
    mode_scale = 0.8
    shared_scale = 0.8
    amplitudes = mode_scale * jax.random.truncated_normal(subkeys[6], -2.5, 2.5, (3, S), jnp.float32)
    shared_amp = shared_scale * jax.random.truncated_normal(subkeys[7], -2.5, 2.5, (S,), jnp.float32)
    smooth = shared_amp * jnp.sin(shared_rates[0] * along_z + shared_rates[1] * along_y + shared_rates[2] * along_x + shared_phase)
    for mode_index in range(3):
        argument = mode_z[mode_index] * along_z + mode_y[mode_index] * along_y + mode_x[mode_index] * along_x + phases[mode_index]
        smooth = smooth + amplitudes[mode_index] * jnp.sin(argument)
    full_shape = (Z, GY, GX, S)
    white_noise = 0.2 * jax.random.truncated_normal(subkeys[8], -4.0, 4.0, full_shape, jnp.float32)
    blocks = Z // ZC
    pairing = jax.random.permutation(subkeys[9], blocks)
    block_of_z = jnp.arange(Z, dtype=jnp.int32) // ZC
    block_of_s = jnp.arange(S, dtype=jnp.int32) // (S // blocks)
    spiked = pairing[block_of_z][:, None] == block_of_s[None, :]
    factor = jnp.where(spiked, 3.0, 1.0)[:, None, None, :]
    return jnp.clip(factor * (smooth + white_noise), -30.0, 30.0).astype(jnp.bfloat16)


def plant(drawn, key, least, top_value):
    index_at = [jax.random.randint(jax.random.fold_in(key, axis), (), 0, length) for axis, length in enumerate(drawn.shape)]
    longest = drawn.shape.index(max(drawn.shape))
    next_to = index_at[:longest] + [(index_at[longest] + 1) % drawn.shape[longest]] + index_at[longest + 1:]
    return drawn.at[tuple(index_at)].set(least).at[tuple(next_to)].set(top_value)


def setup_inputs(seed: int = 0, part: int = 0) -> dict:
    splits = jax.random.split(jax.random.key(seed), 5)
    part_keys = jax.random.split(jax.random.fold_in(splits[4], part), 5)
    snapshots = draw_snapshots(jax.random.fold_in(jax.random.fold_in(splits[4], part), 71), part)
    material = plant(jax.random.randint(part_keys[1], (Z, GY * GX), 0, CLASSES), jax.random.fold_in(part_keys[1], 1), 0, CLASSES - 1).astype(jnp.int32)
    occupancy = plant((jax.random.randint(part_keys[2], (N_BRICKS, TILES), 0, 4) < 3).astype(jnp.int32), jax.random.fold_in(part_keys[2], 1), 0, 1)
    moduli = jnp.clip(jnp.exp(jax.random.uniform(splits[3], (CLASSES,), jnp.float32, math.log(0.19921875), math.log(5.0))), 0.19921875, 5.0).astype(jnp.bfloat16)
    return dict(snapshots=snapshots, material=material, occupancy=occupancy, moduli=moduli)


def stencil(padded_field, padded_modulus):
    depth = padded_field.shape[0] - 2
    rows_y = padded_field.shape[1]
    rows_x = padded_field.shape[2]
    field_full = jnp.pad(padded_field, ((0, 0), (1, 1), (1, 1), (0, 0)))
    modulus_full = jnp.pad(padded_modulus, ((0, 0), (1, 1), (1, 1)))
    center = field_full[1:1 + depth, 1:1 + rows_y, 1:1 + rows_x]
    center_mod = modulus_full[1:1 + depth, 1:1 + rows_y, 1:1 + rows_x]
    mod_sum = jnp.zeros_like(center_mod)
    field_sum = jnp.zeros_like(center)
    product_sum = jnp.zeros_like(center)
    total_weight = 0.0
    for shift_z in (-1, 0, 1):
        for shift_y in (-1, 0, 1):
            for shift_x in (-1, 0, 1):
                nonzero = abs(shift_z) + abs(shift_y) + abs(shift_x)
                if nonzero == 0:
                    continue
                weight = (1.0, 0.5, 0.25)[nonzero - 1]
                total_weight = total_weight + weight
                near = field_full[1 + shift_z:1 + shift_z + depth, 1 + shift_y:1 + shift_y + rows_y, 1 + shift_x:1 + shift_x + rows_x]
                near_mod = modulus_full[1 + shift_z:1 + shift_z + depth, 1 + shift_y:1 + shift_y + rows_y, 1 + shift_x:1 + shift_x + rows_x]
                mod_sum = mod_sum + weight * near_mod
                field_sum = field_sum + weight * near
                product_sum = product_sum + weight * near_mod[..., None] * near
    diagonal = 0.5 * (total_weight * center_mod + mod_sum)
    return diagonal[..., None] * center - 0.5 * center_mod[..., None] * field_sum - 0.5 * product_sum


def reference(snapshots, material, occupancy, moduli):
    tiles = occupancy.reshape(N_BRICKS, GY // 16, GX // 16)
    occupied = jnp.repeat(jnp.repeat(jnp.repeat(tiles, ZC, 0), 16, 1), 16, 2)
    occ_bf = occupied.astype(jnp.bfloat16)
    modulus = moduli[material].reshape(Z, GY, GX) * occ_bf
    field = snapshots * occ_bf[..., None]
    field_pad = jnp.pad(field, ((1, 1), (0, 0), (0, 0), (0, 0)))
    modulus_pad = jnp.pad(modulus, ((1, 1), (0, 0), (0, 0)))

    def one_block(total, block):
        start = (block * ZC).astype(jnp.int32)
        piece = lax.dynamic_slice_in_dim(field_pad, start, ZC + 2, 0).astype(jnp.float32)
        piece_mod = lax.dynamic_slice_in_dim(modulus_pad, start, ZC + 2, 0).astype(jnp.float32)
        image = stencil(piece, piece_mod).astype(jnp.bfloat16).reshape(-1, S)
        own = lax.dynamic_slice_in_dim(field, start, ZC, 0).reshape(-1, S)
        term = lax.dot_general(own.astype(jnp.float32), image.astype(jnp.float32), (((0,), (0,)), ((), ())))
        return total + term, None

    total, _ = lax.scan(one_block, jnp.zeros((S, S), jnp.float32), jnp.arange(N_BRICKS, dtype=jnp.int32))
    return total * (1.0 / VOXELS)
```

```python
import jax
import jax.numpy as jnp
import numpy as np
from jax import lax
from jax.experimental import pallas as pl
from jax.experimental.pallas import tpu as pltpu
from jax.sharding import PartitionSpec as P

BLOCK = 256
EDGE = 128
F32 = jnp.float32
BF16 = jnp.bfloat16


def plane_weights(rows_x):
    source = np.arange(BLOCK + 2 * EDGE) - EDGE
    target = np.arange(BLOCK)
    step_y = np.abs(source[:, None] // rows_x - target[None, :] // rows_x)
    step_x = np.abs(source[:, None] % rows_x - target[None, :] % rows_x)
    weight = np.where(step_y == 0, 1.0, 0.5) * np.where(step_x == 0, 1.0, 0.5)
    weight = np.where((step_y <= 1) & (step_x <= 1), weight, 0.0)
    return jnp.asarray(0.5 * weight, BF16)


def lane_place(shape, rows_x):
    lane = lax.broadcasted_iota(jnp.int32, shape, 1)
    return lane // rows_x, lane % rows_x


def brick_select(occupied, rows_y, rows_x, place_y, place_x):
    o = [occupied(t).astype(F32) for t in range(4)]
    low = jnp.where(place_x < rows_x // 2, o[0], o[1])
    high = jnp.where(place_x < rows_x // 2, o[2], o[3])
    return jnp.where(place_y < rows_y // 2, low, high)


def look_up(material, moduli):
    value = jnp.zeros(material.shape, F32)
    for index in range(moduli.shape[1]):
        value = jnp.where(material == index, moduli[:, index : index + 1], value)
    return value


def smooth_plane(value, rows_y, rows_x):
    place_y, place_x = lane_place(value.shape, rows_x)
    lanes = value.shape[1]
    before = jnp.where(place_x > 0, pltpu.roll(value, 1, 1), 0.0)
    after = jnp.where(place_x < rows_x - 1, pltpu.roll(value, lanes - 1, 1), 0.0)
    value = value + 0.5 * (before + after)
    before = jnp.where(place_y > 0, pltpu.roll(value, rows_x, 1), 0.0)
    after = jnp.where(place_y < rows_y - 1, pltpu.roll(value, lanes - rows_x, 1), 0.0)
    return value + 0.5 * (before + after)


def windows(lanes):
    spans = []
    for start in range(0, lanes, BLOCK):
        low = max(start - EDGE, 0)
        high = min(start + BLOCK + EDGE, lanes)
        spans.append((start, low, high))
    return spans


def mask_weights(weights_ref, masked, occupied, rows_y, rows_x, lanes):
    for number, (start, low, high) in enumerate(windows(lanes)):
        first = low - (start - EDGE)
        shape = (high - low, BLOCK)
        voxel = lax.broadcasted_iota(jnp.int32, shape, 0) + low
        mask = brick_select(occupied, rows_y, rows_x, voxel // rows_x, voxel % rows_x)
        part = weights_ref[first : first + high - low, :].astype(F32) * mask
        masked[number, : high - low, :] = part.astype(BF16)


def pack_kernel(rows_y, rows_x, plane_ref, material_ref, occupied_ref, moduli_ref, out_ref):
    lanes = rows_y * rows_x
    occupied = lambda t: occupied_ref[0, t]
    voxel = lax.broadcasted_iota(jnp.int32, (lanes, plane_ref.shape[-1]), 0)
    mask = brick_select(occupied, rows_y, rows_x, voxel // rows_x, voxel % rows_x)
    out_ref[:lanes, :] = (plane_ref[0].astype(F32) * mask).astype(BF16)
    place_y, place_x = lane_place((8, lanes), rows_x)
    value = look_up(material_ref[...], moduli_ref[...].astype(F32))
    value = value * brick_select(occupied, rows_y, rows_x, place_y, place_x)
    width = out_ref.shape[1]
    for part in range(lanes // width):
        row = value[0:1, part * width : (part + 1) * width]
        start = lanes + 16 * part
        out_ref[start : start + 16, :] = jnp.broadcast_to(row, (16, width)).astype(BF16)


def image_block(ft, smooth, m8, c8, spread):
    rows, lanes = ft.shape
    shape = (rows // 8, 8, lanes)
    field = ft.astype(F32).reshape(shape)
    out = c8[None] * field - m8[None] * smooth.reshape(shape)
    return out.reshape(rows, lanes).astype(BF16)


def main_kernel(
    rows_y, rows_x,
    snapshots_ref, material_ref, occupied_ref, moduli_ref, weights_ref,
    out_ref,
    field, ft, last, pair, image, masked, m8, c8, sems,
):
    depth, lanes, width = snapshots_ref.shape
    occupied = lambda t: occupied_ref[0, t]

    def copy(z):
        return pltpu.make_async_copy(snapshots_ref.at[z], field.at[z], sems.at[z])

    for z in range(depth):
        copy(z).start()

    shape = (depth, lanes)
    place_y, place_x = lane_place(shape, rows_x)
    mask = brick_select(occupied, rows_y, rows_x, place_y, place_x)
    modulus = look_up(material_ref[...], moduli_ref[...].astype(F32)) * mask
    smooth = smooth_plane(modulus, rows_y, rows_x)
    place_z = lax.broadcasted_iota(jnp.int32, shape, 0)
    before = jnp.where(place_z > 0, pltpu.roll(smooth, 1, 0), 0.0)
    after = jnp.where(place_z < depth - 1, pltpu.roll(smooth, depth - 1, 0), 0.0)
    smooth = smooth + 0.5 * (before + after)
    center = (4.0 * modulus + 0.5 * smooth) * mask
    for z in range(depth):
        m8[z] = jnp.broadcast_to(modulus[z : z + 1], (8, lanes))
        c8[z] = jnp.broadcast_to(center[z : z + 1], (8, lanes))
    mask_weights(weights_ref, masked, occupied, rows_y, rows_x, lanes)

    spans = windows(lanes)
    out_ref[...] = jnp.zeros_like(out_ref)

    def smoothed(number, slot):
        start, low, high = spans[number]
        return jnp.dot(
            ft[slot, :, low:high], masked[number, : high - low, :], preferred_element_type=F32
        )

    def emit(z, slot, number, both):
        block = pl.ds(spans[number][0], BLOCK)
        image[:, block] = image_block(
            ft[slot, :, block], both, m8[z, :, block], c8[z, :, block], None
        )

    def gram(z):
        out_ref[...] += jnp.dot(image[...], field[z], preferred_element_type=F32)

    copy(0).wait()
    ft[0] = field[0].T
    for number in range(len(spans)):
        block = pl.ds(spans[number][0], BLOCK)
        new = smoothed(number, 0)
        last[:, block] = new
        pair[:, block] = new

    def step(z, slot):
        copy(z).wait()
        ft[slot] = field[z].T
        for number in range(len(spans)):
            block = pl.ds(spans[number][0], BLOCK)
            new = smoothed(number, slot)
            now = last[:, block] + new
            emit(z - 1, 1 - slot, number, pair[:, block] + now)
            last[:, block] = new
            pair[:, block] = now
        gram(z - 1)

    def two(index, carry):
        z = 2 * index + 1
        step(z, 1)
        step(z + 1, 0)
        return carry

    lax.fori_loop(0, (depth - 2) // 2, two, 0)
    step(depth - 1, 1)
    for number in range(len(spans)):
        block = pl.ds(spans[number][0], BLOCK)
        emit(depth - 1, 1, number, pair[:, block] + last[:, block])
    gram(depth - 1)


def edge_kernel(
    rows_y, rows_x, scale,
    snapshots_ref, halo_ref, material_ref, occupied_ref, moduli_ref, weights_ref, gram_ref,
    out_ref,
    own, masked, image, sem,
):
    depth, lanes, width = snapshots_ref.shape
    occupied = lambda t: occupied_ref[0, t]
    load = pltpu.make_async_copy(snapshots_ref.at[depth - 1], own, sem)
    load.start()
    shape = (8, lanes)
    place_y, place_x = lane_place(shape, rows_x)
    mask = brick_select(occupied, rows_y, rows_x, place_y, place_x)
    value = look_up(material_ref[depth - 8 :, :], moduli_ref[...].astype(F32))
    own_mod = jnp.broadcast_to(value[7:8], shape) * mask
    rows = [
        halo_ref[lanes + 16 * part : lanes + 16 * part + 16, :].astype(F32)[:8]
        for part in range(lanes // width)
    ]
    halo_mod = jnp.concatenate(rows, axis=1)
    own_c = 0.25 * smooth_plane(halo_mod, rows_y, rows_x) * mask
    halo_c = 0.25 * smooth_plane(own_mod, rows_y, rows_x)
    mask_weights(weights_ref, masked, occupied, rows_y, rows_x, lanes)
    halo_t = halo_ref[:lanes, :].T
    load.wait()
    own_t = own[...].T
    for number, (start, low, high) in enumerate(windows(lanes)):
        block = slice(start, start + BLOCK)
        first = low - (start - EDGE)
        from_halo = jnp.dot(
            halo_t[:, low:high], weights_ref[first : first + high - low, :],
            preferred_element_type=F32,
        )
        from_own = jnp.dot(
            own_t[:, low:high], masked[number, : high - low, :], preferred_element_type=F32
        )
        image[0, :, block] = image_block(
            own_t[:, block], from_halo, own_mod[:, block], own_c[:, block], None
        )
        image[1, :, block] = image_block(
            halo_t[:, block], from_own, halo_mod[:, block], halo_c[:, block], None
        )
    total = gram_ref[...]
    total += jnp.dot(image[0], own[...], preferred_element_type=F32)
    total += jnp.dot(image[1], halo_ref[:lanes, :], preferred_element_type=F32)
    out_ref[...] = (total + total.T) * scale


def scatter_sum(value, axis):
    count = lax.axis_size(axis)
    position = lax.axis_index(axis)
    own = value.shape[0] // count
    step = 1
    while step < count:
        value = value.reshape(-1, 2, own, value.shape[-1])
        side = (position // step) % 2
        keep = lax.dynamic_index_in_dim(value, side, 1, keepdims=False)
        give = lax.dynamic_index_in_dim(value, 1 - side, 1, keepdims=False)
        swap = [(device, device ^ step) for device in range(count)]
        value = keep + lax.ppermute(give, axis, swap)
        step *= 2
    return value.reshape(own, value.shape[-1])


def local(snapshots, material, occupancy, moduli):
    depth, rows_y, rows_x, width = snapshots.shape
    lanes = rows_y * rows_x
    owners = lax.axis_size("bricks")
    scale = 1.0 / (depth * lanes * owners)
    planes = snapshots.reshape(depth, lanes, width)
    moduli = moduli.reshape(1, -1)
    weights = plane_weights(rows_x)
    vmem = pl.BlockSpec(memory_space=pltpu.VMEM)
    smem = pl.BlockSpec(memory_space=pltpu.SMEM)
    hbm = pl.BlockSpec(memory_space=pl.ANY)
    spans = len(windows(lanes))
    packed_rows = lanes + 16 * (lanes // width)

    packed = pl.pallas_call(
        lambda *refs: pack_kernel(rows_y, rows_x, *refs),
        grid=(1,),
        in_specs=[
            pl.BlockSpec((1, lanes, width), lambda i: (0, 0, 0)),
            pl.BlockSpec((8, lanes), lambda i: (0, 0)),
            smem,
            pl.BlockSpec(moduli.shape, lambda i: (0, 0)),
        ],
        out_specs=pl.BlockSpec((packed_rows, width), lambda i: (0, 0)),
        out_shape=jax.ShapeDtypeStruct((packed_rows, width), BF16),
        name="pack",
    )(planes, material, occupancy, moduli)

    halo = lax.ppermute(packed, "bricks", [(i + 1, i) for i in range(owners - 1)])

    gram = pl.pallas_call(
        lambda *refs: main_kernel(rows_y, rows_x, *refs),
        in_specs=[hbm, vmem, smem, vmem, vmem],
        out_specs=vmem,
        out_shape=jax.ShapeDtypeStruct((width, width), F32),
        scratch_shapes=[
            pltpu.VMEM((depth, lanes, width), BF16),
            pltpu.VMEM((2, width, lanes), BF16),
            pltpu.VMEM((width, lanes), F32),
            pltpu.VMEM((width, lanes), F32),
            pltpu.VMEM((width, lanes), BF16),
            pltpu.VMEM((spans, BLOCK + 2 * EDGE, BLOCK), BF16),
            pltpu.VMEM((depth, 8, lanes), F32),
            pltpu.VMEM((depth, 8, lanes), F32),
            pltpu.SemaphoreType.DMA((depth,)),
        ],
        compiler_params=pltpu.CompilerParams(vmem_limit_bytes=40 << 20),
        cost_estimate=pl.CostEstimate(
            flops=6 * depth * lanes * width * width,
            bytes_accessed=2 * depth * lanes * width,
            transcendentals=0,
        ),
        name="interior",
    )(planes, material, occupancy, moduli, weights)

    share = pl.pallas_call(
        lambda *refs: edge_kernel(rows_y, rows_x, scale, *refs),
        in_specs=[hbm, vmem, vmem, smem, vmem, vmem, vmem],
        out_specs=vmem,
        out_shape=jax.ShapeDtypeStruct((width, width), F32),
        scratch_shapes=[
            pltpu.VMEM((lanes, width), BF16),
            pltpu.VMEM((spans, BLOCK + 2 * EDGE, BLOCK), BF16),
            pltpu.VMEM((2, width, lanes), BF16),
            pltpu.SemaphoreType.DMA(()),
        ],
        compiler_params=pltpu.CompilerParams(vmem_limit_bytes=32 << 20),
        cost_estimate=pl.CostEstimate(
            flops=12 * lanes * width * width, bytes_accessed=4 * lanes * width, transcendentals=0
        ),
        name="edge",
    )(planes, halo, material, occupancy, moduli, weights, gram)
    return scatter_sum(share, "bricks")


def solution(mesh):
    in_specs = (
        P(("groups", "bricks"), None, None, None),
        P(("groups", "bricks"), None),
        P(("groups", "bricks"), None),
        P(),
    )
    out_specs = P(("groups", "bricks"), None)
    return jax.shard_map(local, mesh=mesh, in_specs=in_specs, out_specs=out_specs, check_vma=False)
```

```python
import jax
import jax.numpy as jnp
import numpy as np
from jax import lax
from jax.experimental import pallas as pl
from jax.experimental.pallas import tpu as pltpu
from jax.sharding import PartitionSpec as P

BLOCK = 256
EDGE = 128
F32 = jnp.float32
BF16 = jnp.bfloat16


def plane_weights(rows_x):
    source = np.arange(BLOCK + 2 * EDGE) - EDGE
    target = np.arange(BLOCK)
    step_y = np.abs(source[:, None] // rows_x - target[None, :] // rows_x)
    step_x = np.abs(source[:, None] % rows_x - target[None, :] % rows_x)
    weight = np.where(step_y == 0, 1.0, 0.5) * np.where(step_x == 0, 1.0, 0.5)
    weight = np.where((step_y <= 1) & (step_x <= 1), weight, 0.0)
    return jnp.asarray(0.5 * weight, BF16)


def lane_place(shape, rows_x):
    lane = lax.broadcasted_iota(jnp.int32, shape, 1)
    return lane // rows_x, lane % rows_x


def brick_select(occupied, rows_y, rows_x, place_y, place_x):
    o = [occupied(t).astype(F32) for t in range(4)]
    low = jnp.where(place_x < rows_x // 2, o[0], o[1])
    high = jnp.where(place_x < rows_x // 2, o[2], o[3])
    return jnp.where(place_y < rows_y // 2, low, high)


def look_up(material, moduli):
    value = jnp.zeros(material.shape, F32)
    for index in range(moduli.shape[1]):
        value = jnp.where(material == index, moduli[:, index : index + 1], value)
    return value


def smooth_plane(value, rows_y, rows_x):
    place_y, place_x = lane_place(value.shape, rows_x)
    lanes = value.shape[1]
    before = jnp.where(place_x > 0, pltpu.roll(value, 1, 1), 0.0)
    after = jnp.where(place_x < rows_x - 1, pltpu.roll(value, lanes - 1, 1), 0.0)
    value = value + 0.5 * (before + after)
    before = jnp.where(place_y > 0, pltpu.roll(value, rows_x, 1), 0.0)
    after = jnp.where(place_y < rows_y - 1, pltpu.roll(value, lanes - rows_x, 1), 0.0)
    return value + 0.5 * (before + after)


def windows(lanes):
    spans = []
    for start in range(0, lanes, BLOCK):
        low = max(start - EDGE, 0)
        high = min(start + BLOCK + EDGE, lanes)
        spans.append((start, low, high))
    return spans


def pack_kernel(
    rows_y, rows_x, snapshots_ref, material_ref, occupied_ref, moduli_ref, out_ref, rows, packed, sems
):
    lanes, width = snapshots_ref.shape[1:]
    plane = pltpu.make_async_copy(snapshots_ref.at[0], out_ref.at[pl.ds(0, lanes)], sems.at[0])
    plane.start()
    occupied = lambda t: occupied_ref[0, t]
    place_y, place_x = lane_place((8, lanes), rows_x)
    value = look_up(material_ref[:8, :], moduli_ref[...].astype(F32))
    value = value * brick_select(occupied, rows_y, rows_x, place_y, place_x)
    rows[...] = jnp.zeros_like(rows)
    for part in range(lanes // width):
        rows[part : part + 1, :] = value[0:1, part * width : (part + 1) * width]
    packed[...] = rows[...].astype(BF16)
    extra = pltpu.make_async_copy(packed, out_ref.at[pl.ds(lanes, 16)], sems.at[1])
    extra.start()
    plane.wait()
    extra.wait()


def main_kernel(
    rows_y, rows_x,
    snapshots_ref, material_ref, occupied_ref, moduli_ref, weights_ref,
    out_ref,
    field, lhs, last, pair, image, modulus_rows, center_columns, masked, sems,
):
    depth, lanes, width = snapshots_ref.shape
    blocks = lanes // BLOCK
    per_block = BLOCK // rows_x
    reach = BLOCK + 2 * rows_x
    occupied = lambda t: occupied_ref[0, t]

    def copy(z):
        return pltpu.make_async_copy(snapshots_ref.at[z], field.at[z], sems.at[z])

    for z in range(depth):
        copy(z).start()

    shape = (depth, lanes)
    place_y, place_x = lane_place(shape, rows_x)
    mask = brick_select(occupied, rows_y, rows_x, place_y, place_x)
    modulus = look_up(material_ref[...], moduli_ref[...].astype(F32)) * mask
    smooth = smooth_plane(modulus, rows_y, rows_x)
    place_z = lax.broadcasted_iota(jnp.int32, shape, 0)
    before = jnp.where(place_z > 0, pltpu.roll(smooth, 1, 0), 0.0)
    after = jnp.where(place_z < depth - 1, pltpu.roll(smooth, depth - 1, 0), 0.0)
    smooth = smooth + 0.5 * (before + after)
    center = (4.0 * modulus + 0.5 * smooth) * mask
    for z in range(depth):
        modulus_rows[z] = jnp.broadcast_to(modulus[z : z + 1], (16, lanes)).astype(BF16)
    center_columns[...] = jnp.concatenate([center, jnp.zeros((128 - depth, lanes), F32)], 0).T
    lhs[...] = jnp.zeros_like(lhs)
    on = [occupied(t) > 0 for t in range(4)]
    for block in range(blocks):
        for row in range(0, reach, 16):
            voxel = min(max(block * BLOCK - rows_x + row, 0), lanes - 16)
            brick = voxel // rows_x // (rows_y // 2) * 2 + voxel % rows_x // (rows_x // 2)
            part = weights_ref[EDGE - rows_x + row : EDGE - rows_x + row + 16, :]
            masked[block, row : row + 16, :] = jnp.where(on[brick], part, jnp.zeros_like(part))
    out_ref[...] = jnp.zeros_like(out_ref)

    half = BLOCK // 2
    span = half + 2 * rows_x

    def smoothed(z, block):
        slot = (z * blocks + block) % 2
        scale = modulus_rows[z, :, block * BLOCK : (block + 1) * BLOCK]
        for side in range(2):
            rows = slice(side * (reach - span), side * (reach - span) + span)
            columns = slice(side * half, (side + 1) * half)
            part = masked[block, rows, columns].reshape(span // 16, 16, half)
            lhs[slot, rows, columns] = (part * scale[None, :, columns]).reshape(span, half)
        return jnp.dot(
            lhs[slot], field[z, block * BLOCK : (block + 1) * BLOCK, :],
            preferred_element_type=F32,
        )

    def plane(z, sink):
        above, below = None, None
        for block in range(blocks):
            value = smoothed(z, block)
            own = [value[rows_x * (i + 1) : rows_x * (i + 2)] for i in range(per_block)]
            if block > 0:
                sink(z, per_block * block - 1, above + value[:rows_x])
                own[0] = own[0] + below
            for i in range(per_block - 1):
                sink(z, per_block * block + i, own[i])
            above, below = own[-1], value[rows_x * (per_block + 1) :]
        sink(z, per_block * blocks - 1, above)

    def start(z, y, new):
        rows = pl.ds(y * rows_x, rows_x)
        last[rows, :] = new
        pair[rows, :] = new

    def emit(z, y, new):
        rows = pl.ds(y * rows_x, rows_x)
        now = last[rows, :] if new is None else last[rows, :] + new
        both = pair[rows, :] + now
        scale = jnp.broadcast_to(center_columns[rows, z - 1 : z], (rows_x, width))
        value = scale * field[z - 1, rows, :].astype(F32) - both
        image[(z - 1) % 2, rows, :] = value.astype(BF16)
        if new is not None:
            last[rows, :] = new
            pair[rows, :] = now

    def gram(z):
        out_ref[...] += jnp.dot(image[z % 2].T, field[z], preferred_element_type=F32)

    copy(0).wait()
    plane(0, start)
    for z in range(1, depth + 1):
        if z >= 2:
            gram(z - 2)
        if z < depth:
            if (z - 1) % 3 == 0:
                for ahead in range(z, min(z + 3, depth)):
                    copy(ahead).wait()
            plane(z, emit)
        else:
            for y in range(rows_y):
                emit(z, y, None)
    gram(depth - 1)


def image_block(ft, smooth, m8, c8):
    rows, lanes = ft.shape
    shape = (rows // 8, 8, lanes)
    field = ft.astype(F32).reshape(shape)
    out = c8[None] * field - m8[None] * smooth.reshape(shape)
    return out.reshape(rows, lanes).astype(BF16)


def edge_kernel(
    rows_y, rows_x, scale,
    snapshots_ref, halo_ref, material_ref, occupied_ref, moduli_ref, weights_ref, gram_ref,
    out_ref,
    own, image, sem,
):
    depth, lanes, width = snapshots_ref.shape
    occupied = lambda t: occupied_ref[0, t]
    load = pltpu.make_async_copy(snapshots_ref.at[depth - 1], own, sem)
    load.start()
    shape = (8, lanes)
    place_y, place_x = lane_place(shape, rows_x)
    own_mask = brick_select(occupied, rows_y, rows_x, place_y, place_x)
    value = look_up(material_ref[depth - 8 :, :], moduli_ref[...].astype(F32))
    own_mod = jnp.broadcast_to(value[7:8], shape) * own_mask
    extra = halo_ref[lanes : lanes + 16, :].astype(F32)
    parts = [extra[part : part + 1, :] for part in range(lanes // width)]
    halo_mod = jnp.broadcast_to(jnp.concatenate(parts, axis=1), shape)
    halo_mask = jnp.where(halo_mod > 0.0, 1.0, 0.0)
    own_c = 0.25 * smooth_plane(halo_mod, rows_y, rows_x) * own_mask
    halo_c = 0.25 * smooth_plane(own_mod, rows_y, rows_x) * halo_mask
    halo_t = halo_ref[:lanes, :].T
    halo_on = halo_t * halo_mask[0:1].astype(BF16)
    load.wait()
    own_t = own[...].T
    own_on = own_t * own_mask[0:1].astype(BF16)
    for start, low, high in windows(lanes):
        block = slice(start, start + BLOCK)
        first = low - (start - EDGE)
        part = weights_ref[first : first + high - low, :]
        from_halo = jnp.dot(halo_on[:, low:high], part, preferred_element_type=F32)
        from_own = jnp.dot(own_on[:, low:high], part, preferred_element_type=F32)
        image[0, :, block] = image_block(
            own_t[:, block], from_halo, own_mod[:, block], own_c[:, block]
        )
        image[1, :, block] = image_block(
            halo_t[:, block], from_own, halo_mod[:, block], halo_c[:, block]
        )
    total = gram_ref[...]
    total += jnp.dot(image[0], own[...], preferred_element_type=F32)
    total += jnp.dot(image[1], halo_ref[:lanes, :], preferred_element_type=F32)
    out_ref[...] = (total + total.T) * scale


def scatter_sum(value, axis):
    count = lax.axis_size(axis)
    position = lax.axis_index(axis)
    own = value.shape[0] // count
    step = 1
    while step < count:
        value = value.reshape(-1, 2, own, value.shape[-1])
        side = (position // step) % 2
        keep = lax.dynamic_index_in_dim(value, side, 1, keepdims=False)
        give = lax.dynamic_index_in_dim(value, 1 - side, 1, keepdims=False)
        swap = [(device, device ^ step) for device in range(count)]
        value = keep + lax.ppermute(give, axis, swap)
        step *= 2
    return value.reshape(own, value.shape[-1])


def local(snapshots, material, occupancy, moduli):
    depth, rows_y, rows_x, width = snapshots.shape
    lanes = rows_y * rows_x
    owners = lax.axis_size("bricks")
    scale = 1.0 / (depth * lanes * owners)
    planes = snapshots.reshape(depth, lanes, width)
    moduli = moduli.reshape(1, -1)
    weights = plane_weights(rows_x)
    vmem = pl.BlockSpec(memory_space=pltpu.VMEM)
    smem = pl.BlockSpec(memory_space=pltpu.SMEM)
    hbm = pl.BlockSpec(memory_space=pltpu.HBM)
    reach = BLOCK + 2 * rows_x

    packed = pl.pallas_call(
        lambda *refs: pack_kernel(rows_y, rows_x, *refs),
        in_specs=[hbm, vmem, smem, vmem],
        out_specs=hbm,
        out_shape=jax.ShapeDtypeStruct((lanes + 16, width), BF16),
        scratch_shapes=[
            pltpu.VMEM((16, width), F32),
            pltpu.VMEM((16, width), BF16),
            pltpu.SemaphoreType.DMA((2,)),
        ],
        compiler_params=pltpu.CompilerParams(vmem_limit_bytes=56 << 20),
        name="pack",
    )(planes, material, occupancy, moduli)

    halo = lax.ppermute(packed, "bricks", [(i + 1, i) for i in range(owners - 1)])

    gram = pl.pallas_call(
        lambda *refs: main_kernel(rows_y, rows_x, *refs),
        in_specs=[hbm, vmem, smem, vmem, vmem],
        out_specs=vmem,
        out_shape=jax.ShapeDtypeStruct((width, width), F32),
        scratch_shapes=[
            pltpu.VMEM((depth, lanes, width), BF16),
            pltpu.VMEM((2, reach, BLOCK), BF16),
            pltpu.VMEM((lanes, width), F32),
            pltpu.VMEM((lanes, width), F32),
            pltpu.VMEM((2, lanes, width), BF16),
            pltpu.VMEM((depth, 16, lanes), BF16),
            pltpu.VMEM((lanes, 128), F32),
            pltpu.VMEM((lanes // BLOCK, reach, BLOCK), BF16),
            pltpu.SemaphoreType.DMA((depth,)),
        ],
        compiler_params=pltpu.CompilerParams(vmem_limit_bytes=56 << 20),
        cost_estimate=pl.CostEstimate(
            flops=6 * depth * lanes * width * width,
            bytes_accessed=2 * depth * lanes * width,
            transcendentals=0,
        ),
        name="interior",
    )(planes, material, occupancy, moduli, weights)

    share = pl.pallas_call(
        lambda *refs: edge_kernel(rows_y, rows_x, scale, *refs),
        in_specs=[hbm, vmem, vmem, smem, vmem, vmem, vmem],
        out_specs=vmem,
        out_shape=jax.ShapeDtypeStruct((width, width), F32),
        scratch_shapes=[
            pltpu.VMEM((lanes, width), BF16),
            pltpu.VMEM((2, width, lanes), BF16),
            pltpu.SemaphoreType.DMA(()),
        ],
        compiler_params=pltpu.CompilerParams(vmem_limit_bytes=24 << 20),
        cost_estimate=pl.CostEstimate(
            flops=12 * lanes * width * width, bytes_accessed=4 * lanes * width, transcendentals=0
        ),
        name="edge",
    )(planes, halo, material, occupancy, moduli, weights, gram)
    return scatter_sum(share, "bricks")


def solution(mesh):
    in_specs = (
        P(("groups", "bricks"), None, None, None),
        P(("groups", "bricks"), None),
        P(("groups", "bricks"), None),
        P(),
    )
    out_specs = P(("groups", "bricks"), None)
    return jax.shard_map(local, mesh=mesh, in_specs=in_specs, out_specs=out_specs, check_vma=False)
```

```python
import jax
import jax.numpy as jnp
import numpy as np
from jax import lax
from jax.experimental import pallas as pl
from jax.experimental.pallas import tpu as pltpu
from jax.sharding import PartitionSpec as P

BLOCK = 256
EDGE = 128
F32 = jnp.float32
BF16 = jnp.bfloat16


def plane_weights(rows_x):
    source = np.arange(BLOCK + 2 * EDGE) - EDGE
    target = np.arange(BLOCK)
    step_y = np.abs(source[:, None] // rows_x - target[None, :] // rows_x)
    step_x = np.abs(source[:, None] % rows_x - target[None, :] % rows_x)
    weight = np.where(step_y == 0, 1.0, 0.5) * np.where(step_x == 0, 1.0, 0.5)
    weight = np.where((step_y <= 1) & (step_x <= 1), weight, 0.0)
    return jnp.asarray(0.5 * weight, BF16)


def lane_place(shape, rows_x):
    lane = lax.broadcasted_iota(jnp.int32, shape, 1)
    return lane // rows_x, lane % rows_x


def brick_select(occupied, rows_y, rows_x, place_y, place_x):
    o = [occupied(t).astype(F32) for t in range(4)]
    low = jnp.where(place_x < rows_x // 2, o[0], o[1])
    high = jnp.where(place_x < rows_x // 2, o[2], o[3])
    return jnp.where(place_y < rows_y // 2, low, high)


def look_up(material, moduli):
    value = jnp.zeros(material.shape, F32)
    for index in range(moduli.shape[1]):
        value = jnp.where(material == index, moduli[:, index : index + 1], value)
    return value


def smooth_plane(value, rows_y, rows_x):
    place_y, place_x = lane_place(value.shape, rows_x)
    lanes = value.shape[1]
    before = jnp.where(place_x > 0, pltpu.roll(value, 1, 1), 0.0)
    after = jnp.where(place_x < rows_x - 1, pltpu.roll(value, lanes - 1, 1), 0.0)
    value = value + 0.5 * (before + after)
    before = jnp.where(place_y > 0, pltpu.roll(value, rows_x, 1), 0.0)
    after = jnp.where(place_y < rows_y - 1, pltpu.roll(value, lanes - rows_x, 1), 0.0)
    return value + 0.5 * (before + after)


def windows(lanes):
    spans = []
    for start in range(0, lanes, BLOCK):
        low = max(start - EDGE, 0)
        high = min(start + BLOCK + EDGE, lanes)
        spans.append((start, low, high))
    return spans


def pack_kernel(
    rows_y, rows_x, snapshots_ref, material_ref, occupied_ref, moduli_ref, out_ref, rows, sem
):
    lanes, width = snapshots_ref.shape[1:]
    plane = pltpu.make_async_copy(snapshots_ref.at[0], out_ref.at[pl.ds(0, lanes)], sem)
    plane.start()
    occupied = lambda t: occupied_ref[0, t]
    place_y, place_x = lane_place((8, lanes), rows_x)
    value = look_up(material_ref[:8, :], moduli_ref[...].astype(F32))
    value = value * brick_select(occupied, rows_y, rows_x, place_y, place_x)
    rows[...] = jnp.zeros_like(rows)
    for part in range(lanes // width):
        rows[part : part + 1, :] = value[0:1, part * width : (part + 1) * width]
    out_ref[lanes : lanes + 16, :] = rows[...].astype(BF16)
    plane.wait()


def main_kernel(
    rows_y, rows_x,
    snapshots_ref, material_ref, occupied_ref, moduli_ref, weights_ref,
    out_ref, top_ref,
    field, lhs, last, pair, image, modulus_rows, center_columns, masked, sems, top_sem,
):
    depth, lanes, width = snapshots_ref.shape
    blocks = lanes // BLOCK
    per_block = BLOCK // rows_x
    reach = BLOCK + 2 * rows_x
    occupied = lambda t: occupied_ref[0, t]

    def copy(z):
        return pltpu.make_async_copy(snapshots_ref.at[z], field.at[z], sems.at[z])

    for z in range(depth):
        copy(z).start()

    shape = (depth, lanes)
    place_y, place_x = lane_place(shape, rows_x)
    mask = brick_select(occupied, rows_y, rows_x, place_y, place_x)
    modulus = look_up(material_ref[...], moduli_ref[...].astype(F32)) * mask
    smooth = smooth_plane(modulus, rows_y, rows_x)
    place_z = lax.broadcasted_iota(jnp.int32, shape, 0)
    before = jnp.where(place_z > 0, pltpu.roll(smooth, 1, 0), 0.0)
    after = jnp.where(place_z < depth - 1, pltpu.roll(smooth, depth - 1, 0), 0.0)
    smooth = smooth + 0.5 * (before + after)
    center = (4.0 * modulus + 0.5 * smooth) * mask
    for z in range(depth):
        modulus_rows[z] = jnp.broadcast_to(modulus[z : z + 1], (16, lanes)).astype(BF16)
    center_columns[...] = jnp.concatenate([center, jnp.zeros((128 - depth, lanes), F32)], 0).T
    lhs[...] = jnp.zeros_like(lhs)
    on = [occupied(t) > 0 for t in range(4)]
    for block in range(blocks):
        for row in range(0, reach, 16):
            voxel = min(max(block * BLOCK - rows_x + row, 0), lanes - 16)
            brick = voxel // rows_x // (rows_y // 2) * 2 + voxel % rows_x // (rows_x // 2)
            part = weights_ref[EDGE - rows_x + row : EDGE - rows_x + row + 16, :]
            masked[block, row : row + 16, :] = jnp.where(on[brick], part, jnp.zeros_like(part))
    out_ref[...] = jnp.zeros_like(out_ref)

    half = BLOCK // 2
    span = half + 2 * rows_x

    def smoothed(z, block):
        slot = (z * blocks + block) % 2
        scale = modulus_rows[z, :, block * BLOCK : (block + 1) * BLOCK]
        for side in range(2):
            rows = slice(side * (reach - span), side * (reach - span) + span)
            columns = slice(side * half, (side + 1) * half)
            part = masked[block, rows, columns].reshape(span // 16, 16, half)
            lhs[slot, rows, columns] = (part * scale[None, :, columns]).reshape(span, half)
        return jnp.dot(
            lhs[slot], field[z, block * BLOCK : (block + 1) * BLOCK, :],
            preferred_element_type=F32,
        )

    def plane(z, sink):
        above, below = None, None
        for block in range(blocks):
            value = smoothed(z, block)
            own = [value[rows_x * (i + 1) : rows_x * (i + 2)] for i in range(per_block)]
            if block > 0:
                sink(z, per_block * block - 1, above + value[:rows_x])
                own[0] = own[0] + below
            for i in range(per_block - 1):
                sink(z, per_block * block + i, own[i])
            above, below = own[-1], value[rows_x * (per_block + 1) :]
        sink(z, per_block * blocks - 1, above)

    def start(z, y, new):
        rows = pl.ds(y * rows_x, rows_x)
        last[rows, :] = new
        pair[rows, :] = new

    def emit(z, y, new):
        rows = pl.ds(y * rows_x, rows_x)
        now = last[rows, :] if new is None else last[rows, :] + new
        both = pair[rows, :] + now
        scale = jnp.broadcast_to(center_columns[rows, z - 1 : z], (rows_x, width))
        value = scale * field[z - 1, rows, :].astype(F32) - both
        image[(z - 1) % 2, rows, :] = value.astype(BF16)
        if new is not None:
            last[rows, :] = new
            pair[rows, :] = now

    def gram(z):
        out_ref[...] += jnp.dot(image[z % 2].T, field[z], preferred_element_type=F32)

    top = pltpu.make_async_copy(field.at[depth - 1], top_ref, top_sem)
    copy(0).wait()
    plane(0, start)
    for z in range(1, depth + 1):
        if z >= 2:
            gram(z - 2)
        if z < depth:
            if (z - 1) % 3 == 0:
                for ahead in range(z, min(z + 3, depth)):
                    copy(ahead).wait()
                    if ahead == depth - 1:
                        top.start()
            plane(z, emit)
        else:
            for y in range(rows_y):
                emit(z, y, None)
    gram(depth - 1)
    top.wait()


def image_block(ft, smooth, m8, c8):
    rows, lanes = ft.shape
    shape = (rows // 8, 8, lanes)
    field = ft.astype(F32).reshape(shape)
    out = c8[None] * field - m8[None] * smooth.reshape(shape)
    return out.reshape(rows, lanes).astype(BF16)


def edge_kernel(
    rows_y, rows_x, scale,
    own, halo_ref, material_ref, occupied_ref, moduli_ref, weights_ref, gram_ref,
    out_ref,
    image,
):
    lanes, width = own.shape
    depth = material_ref.shape[0]
    occupied = lambda t: occupied_ref[0, t]
    shape = (8, lanes)
    place_y, place_x = lane_place(shape, rows_x)
    own_mask = brick_select(occupied, rows_y, rows_x, place_y, place_x)
    value = look_up(material_ref[depth - 8 :, :], moduli_ref[...].astype(F32))
    own_mod = jnp.broadcast_to(value[7:8], shape) * own_mask
    extra = halo_ref[lanes : lanes + 16, :].astype(F32)
    parts = [extra[part : part + 1, :] for part in range(lanes // width)]
    halo_mod = jnp.broadcast_to(jnp.concatenate(parts, axis=1), shape)
    halo_mask = jnp.where(halo_mod > 0.0, 1.0, 0.0)
    own_c = 0.25 * smooth_plane(halo_mod, rows_y, rows_x) * own_mask
    halo_c = 0.25 * smooth_plane(own_mod, rows_y, rows_x) * halo_mask
    halo_t = halo_ref[:lanes, :].T
    halo_on = halo_t * halo_mask[0:1].astype(BF16)
    own_t = own[...].T
    own_on = own_t * own_mask[0:1].astype(BF16)
    for start, low, high in windows(lanes):
        block = slice(start, start + BLOCK)
        first = low - (start - EDGE)
        part = weights_ref[first : first + high - low, :]
        from_halo = jnp.dot(halo_on[:, low:high], part, preferred_element_type=F32)
        from_own = jnp.dot(own_on[:, low:high], part, preferred_element_type=F32)
        image[0, :, block] = image_block(
            own_t[:, block], from_halo, own_mod[:, block], own_c[:, block]
        )
        image[1, :, block] = image_block(
            halo_t[:, block], from_own, halo_mod[:, block], halo_c[:, block]
        )
    total = gram_ref[...]
    total += jnp.dot(image[0], own[...], preferred_element_type=F32)
    total += jnp.dot(image[1], halo_ref[:lanes, :], preferred_element_type=F32)
    out_ref[...] = (total + total.T) * scale


def scatter_sum(value, axis):
    count = lax.axis_size(axis)
    position = lax.axis_index(axis)
    own = value.shape[0] // count
    step = 1
    while step < count:
        value = value.reshape(-1, 2, own, value.shape[-1])
        side = (position // step) % 2
        keep = lax.dynamic_index_in_dim(value, side, 1, keepdims=False)
        give = lax.dynamic_index_in_dim(value, 1 - side, 1, keepdims=False)
        swap = [(device, device ^ step) for device in range(count)]
        value = keep + lax.ppermute(give, axis, swap)
        step *= 2
    return value.reshape(own, value.shape[-1])


def local(snapshots, material, occupancy, moduli):
    depth, rows_y, rows_x, width = snapshots.shape
    lanes = rows_y * rows_x
    owners = lax.axis_size("bricks")
    scale = 1.0 / (depth * lanes * owners)
    planes = snapshots.reshape(depth, lanes, width)
    moduli = moduli.reshape(1, -1)
    weights = plane_weights(rows_x)
    vmem = pl.BlockSpec(memory_space=pltpu.VMEM)
    smem = pl.BlockSpec(memory_space=pltpu.SMEM)
    hbm = pl.BlockSpec(memory_space=pltpu.HBM)
    reach = BLOCK + 2 * rows_x

    packed = pl.pallas_call(
        lambda *refs: pack_kernel(rows_y, rows_x, *refs),
        in_specs=[hbm, vmem, smem, vmem],
        out_specs=vmem,
        out_shape=jax.ShapeDtypeStruct((lanes + 16, width), BF16),
        scratch_shapes=[pltpu.VMEM((16, width), F32), pltpu.SemaphoreType.DMA(())],
        compiler_params=pltpu.CompilerParams(vmem_limit_bytes=52 << 20),
        name="pack",
    )(planes, material, occupancy, moduli)

    halo = lax.ppermute(packed, "bricks", [(i + 1, i) for i in range(owners - 1)])

    gram, top = pl.pallas_call(
        lambda *refs: main_kernel(rows_y, rows_x, *refs),
        in_specs=[hbm, vmem, smem, vmem, vmem],
        out_specs=(vmem, hbm),
        out_shape=(
            jax.ShapeDtypeStruct((width, width), F32),
            jax.ShapeDtypeStruct((lanes, width), BF16),
        ),
        scratch_shapes=[
            pltpu.VMEM((depth, lanes, width), BF16),
            pltpu.VMEM((2, reach, BLOCK), BF16),
            pltpu.VMEM((lanes, width), F32),
            pltpu.VMEM((lanes, width), F32),
            pltpu.VMEM((2, lanes, width), BF16),
            pltpu.VMEM((depth, 16, lanes), BF16),
            pltpu.VMEM((lanes, 128), F32),
            pltpu.VMEM((lanes // BLOCK, reach, BLOCK), BF16),
            pltpu.SemaphoreType.DMA((depth,)),
            pltpu.SemaphoreType.DMA(()),
        ],
        compiler_params=pltpu.CompilerParams(vmem_limit_bytes=52 << 20),
        cost_estimate=pl.CostEstimate(
            flops=6 * depth * lanes * width * width,
            bytes_accessed=2 * depth * lanes * width,
            transcendentals=0,
        ),
        name="interior",
    )(planes, material, occupancy, moduli, weights)

    share = pl.pallas_call(
        lambda *refs: edge_kernel(rows_y, rows_x, scale, *refs),
        in_specs=[vmem, vmem, vmem, smem, vmem, vmem, vmem],
        out_specs=vmem,
        out_shape=jax.ShapeDtypeStruct((width, width), F32),
        scratch_shapes=[pltpu.VMEM((2, width, lanes), BF16)],
        compiler_params=pltpu.CompilerParams(vmem_limit_bytes=40 << 20),
        cost_estimate=pl.CostEstimate(
            flops=12 * lanes * width * width, bytes_accessed=4 * lanes * width, transcendentals=0
        ),
        name="edge",
    )(top, halo, material, occupancy, moduli, weights, gram)
    return scatter_sum(share, "bricks")


def solution(mesh):
    in_specs = (
        P(("groups", "bricks"), None, None, None),
        P(("groups", "bricks"), None),
        P(("groups", "bricks"), None),
        P(),
    )
    out_specs = P(("groups", "bricks"), None)
    return jax.shard_map(local, mesh=mesh, in_specs=in_specs, out_specs=out_specs, check_vma=False)
```

```python
import jax
import jax.numpy as jnp
import numpy as np
from jax import lax
from jax.experimental import pallas as pl
from jax.experimental.pallas import tpu as pltpu
from jax.sharding import PartitionSpec as P

BLOCK = 256
EDGE = 128
F32 = jnp.float32
BF16 = jnp.bfloat16


def plane_weights(rows_x):
    source = np.arange(BLOCK + 2 * EDGE) - EDGE
    target = np.arange(BLOCK)
    step_y = np.abs(source[:, None] // rows_x - target[None, :] // rows_x)
    step_x = np.abs(source[:, None] % rows_x - target[None, :] % rows_x)
    weight = np.where(step_y == 0, 1.0, 0.5) * np.where(step_x == 0, 1.0, 0.5)
    weight = np.where((step_y <= 1) & (step_x <= 1), weight, 0.0)
    return jnp.asarray(0.5 * weight, BF16)


def lane_place(shape, rows_x):
    lane = lax.broadcasted_iota(jnp.int32, shape, 1)
    return lane // rows_x, lane % rows_x


def brick_select(occupied, rows_y, rows_x, place_y, place_x):
    o = [occupied(t).astype(F32) for t in range(4)]
    low = jnp.where(place_x < rows_x // 2, o[0], o[1])
    high = jnp.where(place_x < rows_x // 2, o[2], o[3])
    return jnp.where(place_y < rows_y // 2, low, high)


def look_up(material, moduli):
    value = jnp.zeros(material.shape, F32)
    for index in range(moduli.shape[1]):
        value = jnp.where(material == index, moduli[:, index : index + 1], value)
    return value


def smooth_plane(value, rows_y, rows_x):
    place_y, place_x = lane_place(value.shape, rows_x)
    lanes = value.shape[1]
    before = jnp.where(place_x > 0, pltpu.roll(value, 1, 1), 0.0)
    after = jnp.where(place_x < rows_x - 1, pltpu.roll(value, lanes - 1, 1), 0.0)
    value = value + 0.5 * (before + after)
    before = jnp.where(place_y > 0, pltpu.roll(value, rows_x, 1), 0.0)
    after = jnp.where(place_y < rows_y - 1, pltpu.roll(value, lanes - rows_x, 1), 0.0)
    return value + 0.5 * (before + after)


def windows(lanes):
    spans = []
    for start in range(0, lanes, BLOCK):
        low = max(start - EDGE, 0)
        high = min(start + BLOCK + EDGE, lanes)
        spans.append((start, low, high))
    return spans


def pack_kernel(
    rows_y, rows_x,
    snapshots_ref, material_hbm, occupied_hbm, moduli_hbm,
    out_ref,
    material_ref, occupied_ref, moduli_ref, plane_ref, rows, sems,
):
    lanes, width = snapshots_ref.shape[1:]
    copies = [
        pltpu.make_async_copy(source, target, sems.at[number])
        for number, (source, target) in enumerate((
            (material_hbm.at[pl.ds(0, 8)], material_ref),
            (occupied_hbm, occupied_ref),
            (moduli_hbm, moduli_ref),
            (snapshots_ref.at[0], plane_ref.at[pl.ds(0, lanes)]),
        ))
    ]
    for copy in copies:
        copy.start()
    for copy in copies[:3]:
        copy.wait()
    occupied = lambda t: occupied_ref[0, t]
    place_y, place_x = lane_place((8, lanes), rows_x)
    value = look_up(material_ref[...], moduli_ref[...].astype(F32))
    value = value * brick_select(occupied, rows_y, rows_x, place_y, place_x)
    rows[...] = jnp.zeros_like(rows)
    for part in range(lanes // width):
        rows[part : part + 1, :] = value[0:1, part * width : (part + 1) * width]
    plane_ref[lanes : lanes + 16, :] = rows[...].astype(BF16)
    copies[3].wait()
    send = pltpu.make_async_copy(plane_ref, out_ref, sems.at[4])
    send.start()
    send.wait()


def main_kernel(
    rows_y, rows_x,
    snapshots_ref, material_ref, occupied_ref, moduli_ref, weights_ref,
    out_ref, top_ref,
    field, lhs, last, pair, image, modulus_rows, center_columns, masked, sems, top_sem,
):
    depth, lanes, width = snapshots_ref.shape
    blocks = lanes // BLOCK
    per_block = BLOCK // rows_x
    reach = BLOCK + 2 * rows_x
    occupied = lambda t: occupied_ref[0, t]

    def copy(z):
        return pltpu.make_async_copy(snapshots_ref.at[z], field.at[z], sems.at[z])

    for z in range(depth):
        copy(z).start()

    shape = (depth, lanes)
    place_y, place_x = lane_place(shape, rows_x)
    mask = brick_select(occupied, rows_y, rows_x, place_y, place_x)
    modulus = look_up(material_ref[...], moduli_ref[...].astype(F32)) * mask
    smooth = smooth_plane(modulus, rows_y, rows_x)
    place_z = lax.broadcasted_iota(jnp.int32, shape, 0)
    before = jnp.where(place_z > 0, pltpu.roll(smooth, 1, 0), 0.0)
    after = jnp.where(place_z < depth - 1, pltpu.roll(smooth, depth - 1, 0), 0.0)
    smooth = smooth + 0.5 * (before + after)
    center = (4.0 * modulus + 0.5 * smooth) * mask
    for z in range(depth):
        modulus_rows[z] = jnp.broadcast_to(modulus[z : z + 1], (16, lanes)).astype(BF16)
    center_columns[...] = jnp.concatenate([center, jnp.zeros((128 - depth, lanes), F32)], 0).T
    lhs[...] = jnp.zeros_like(lhs)
    on = [occupied(t) > 0 for t in range(4)]
    for block in range(blocks):
        for row in range(0, reach, 16):
            voxel = min(max(block * BLOCK - rows_x + row, 0), lanes - 16)
            brick = voxel // rows_x // (rows_y // 2) * 2 + voxel % rows_x // (rows_x // 2)
            part = weights_ref[EDGE - rows_x + row : EDGE - rows_x + row + 16, :]
            masked[block, row : row + 16, :] = jnp.where(on[brick], part, jnp.zeros_like(part))
    out_ref[...] = jnp.zeros_like(out_ref)

    half = BLOCK // 2
    span = half + 2 * rows_x

    def smoothed(z, block):
        slot = (z * blocks + block) % 2
        scale = modulus_rows[z, :, block * BLOCK : (block + 1) * BLOCK]
        for side in range(2):
            rows = slice(side * (reach - span), side * (reach - span) + span)
            columns = slice(side * half, (side + 1) * half)
            part = masked[block, rows, columns].reshape(span // 16, 16, half)
            lhs[slot, rows, columns] = (part * scale[None, :, columns]).reshape(span, half)
        return jnp.dot(
            lhs[slot], field[z, block * BLOCK : (block + 1) * BLOCK, :],
            preferred_element_type=F32,
        )

    def plane(z, sink):
        above, below = None, None
        for block in range(blocks):
            value = smoothed(z, block)
            own = [value[rows_x * (i + 1) : rows_x * (i + 2)] for i in range(per_block)]
            if block > 0:
                sink(z, per_block * block - 1, above + value[:rows_x])
                own[0] = own[0] + below
            for i in range(per_block - 1):
                sink(z, per_block * block + i, own[i])
            above, below = own[-1], value[rows_x * (per_block + 1) :]
        sink(z, per_block * blocks - 1, above)

    def start(z, y, new):
        rows = pl.ds(y * rows_x, rows_x)
        last[rows, :] = new
        pair[rows, :] = new

    def emit(z, y, new):
        rows = pl.ds(y * rows_x, rows_x)
        now = last[rows, :] if new is None else last[rows, :] + new
        both = pair[rows, :] + now
        scale = jnp.broadcast_to(center_columns[rows, z - 1 : z], (rows_x, width))
        value = scale * field[z - 1, rows, :].astype(F32) - both
        image[(z - 1) % 2, rows, :] = value.astype(BF16)
        if new is not None:
            last[rows, :] = new
            pair[rows, :] = now

    def gram(z):
        out_ref[...] += jnp.dot(image[z % 2].T, field[z], preferred_element_type=F32)

    top = pltpu.make_async_copy(field.at[depth - 1], top_ref, top_sem)
    copy(0).wait()
    plane(0, start)
    for z in range(1, depth + 1):
        if z >= 2:
            gram(z - 2)
        if z < depth:
            if (z - 1) % 3 == 0:
                for ahead in range(z, min(z + 3, depth)):
                    copy(ahead).wait()
                    if ahead == depth - 1:
                        top.start()
            plane(z, emit)
        else:
            for y in range(rows_y):
                emit(z, y, None)
    gram(depth - 1)
    top.wait()


def image_block(ft, smooth, m8, c8):
    rows, lanes = ft.shape
    shape = (rows // 8, 8, lanes)
    field = ft.astype(F32).reshape(shape)
    out = c8[None] * field - m8[None] * smooth.reshape(shape)
    return out.reshape(rows, lanes).astype(BF16)


def edge_kernel(
    rows_y, rows_x, scale,
    own, halo_ref, material_ref, occupied_ref, moduli_ref, weights_ref, gram_ref,
    out_ref,
    image,
):
    lanes, width = own.shape
    depth = material_ref.shape[0]
    occupied = lambda t: occupied_ref[0, t]
    shape = (8, lanes)
    place_y, place_x = lane_place(shape, rows_x)
    own_mask = brick_select(occupied, rows_y, rows_x, place_y, place_x)
    value = look_up(material_ref[depth - 8 :, :], moduli_ref[...].astype(F32))
    own_mod = jnp.broadcast_to(value[7:8], shape) * own_mask
    extra = halo_ref[lanes : lanes + 16, :].astype(F32)
    parts = [extra[part : part + 1, :] for part in range(lanes // width)]
    halo_mod = jnp.broadcast_to(jnp.concatenate(parts, axis=1), shape)
    halo_mask = jnp.where(halo_mod > 0.0, 1.0, 0.0)
    own_c = 0.25 * smooth_plane(halo_mod, rows_y, rows_x) * own_mask
    halo_c = 0.25 * smooth_plane(own_mod, rows_y, rows_x) * halo_mask
    halo_t = halo_ref[:lanes, :].T
    halo_on = halo_t * halo_mask[0:1].astype(BF16)
    own_t = own[...].T
    own_on = own_t * own_mask[0:1].astype(BF16)
    for start, low, high in windows(lanes):
        block = slice(start, start + BLOCK)
        first = low - (start - EDGE)
        part = weights_ref[first : first + high - low, :]
        from_halo = jnp.dot(halo_on[:, low:high], part, preferred_element_type=F32)
        from_own = jnp.dot(own_on[:, low:high], part, preferred_element_type=F32)
        image[0, :, block] = image_block(
            own_t[:, block], from_halo, own_mod[:, block], own_c[:, block]
        )
        image[1, :, block] = image_block(
            halo_t[:, block], from_own, halo_mod[:, block], halo_c[:, block]
        )
    total = gram_ref[...]
    total += jnp.dot(image[0], own[...], preferred_element_type=F32)
    total += jnp.dot(image[1], halo_ref[:lanes, :], preferred_element_type=F32)
    out_ref[...] = (total + total.T) * scale


def scatter_sum(value, axis):
    count = lax.axis_size(axis)
    position = lax.axis_index(axis)
    own = value.shape[0] // count
    step = 1
    while step < count:
        value = value.reshape(-1, 2, own, value.shape[-1])
        side = (position // step) % 2
        keep = lax.dynamic_index_in_dim(value, side, 1, keepdims=False)
        give = lax.dynamic_index_in_dim(value, 1 - side, 1, keepdims=False)
        swap = [(device, device ^ step) for device in range(count)]
        value = keep + lax.ppermute(give, axis, swap)
        step *= 2
    return value.reshape(own, value.shape[-1])


def local(snapshots, material, occupancy, moduli):
    depth, rows_y, rows_x, width = snapshots.shape
    lanes = rows_y * rows_x
    owners = lax.axis_size("bricks")
    scale = 1.0 / (depth * lanes * owners)
    planes = snapshots.reshape(depth, lanes, width)
    moduli = moduli.reshape(1, -1)
    weights = plane_weights(rows_x)
    vmem = pl.BlockSpec(memory_space=pltpu.VMEM)
    smem = pl.BlockSpec(memory_space=pltpu.SMEM)
    hbm = pl.BlockSpec(memory_space=pltpu.HBM)
    reach = BLOCK + 2 * rows_x

    packed = pl.pallas_call(
        lambda *refs: pack_kernel(rows_y, rows_x, *refs),
        in_specs=[hbm, hbm, hbm, hbm],
        out_specs=hbm,
        out_shape=jax.ShapeDtypeStruct((lanes + 16, width), BF16),
        scratch_shapes=[
            pltpu.VMEM((8, lanes), material.dtype),
            pltpu.SMEM(occupancy.shape, occupancy.dtype),
            pltpu.VMEM(moduli.shape, moduli.dtype),
            pltpu.VMEM((lanes + 16, width), BF16),
            pltpu.VMEM((16, width), F32),
            pltpu.SemaphoreType.DMA((5,)),
        ],
        compiler_params=pltpu.CompilerParams(vmem_limit_bytes=56 << 20),
        name="pack",
    )(planes, material, occupancy, moduli)

    halo = lax.ppermute(packed, "bricks", [(i + 1, i) for i in range(owners - 1)])

    gram, top = pl.pallas_call(
        lambda *refs: main_kernel(rows_y, rows_x, *refs),
        in_specs=[hbm, vmem, smem, vmem, vmem],
        out_specs=(vmem, hbm),
        out_shape=(
            jax.ShapeDtypeStruct((width, width), F32),
            jax.ShapeDtypeStruct((lanes, width), BF16),
        ),
        scratch_shapes=[
            pltpu.VMEM((depth, lanes, width), BF16),
            pltpu.VMEM((2, reach, BLOCK), BF16),
            pltpu.VMEM((lanes, width), F32),
            pltpu.VMEM((lanes, width), F32),
            pltpu.VMEM((2, lanes, width), BF16),
            pltpu.VMEM((depth, 16, lanes), BF16),
            pltpu.VMEM((lanes, 128), F32),
            pltpu.VMEM((lanes // BLOCK, reach, BLOCK), BF16),
            pltpu.SemaphoreType.DMA((depth,)),
            pltpu.SemaphoreType.DMA(()),
        ],
        compiler_params=pltpu.CompilerParams(vmem_limit_bytes=52 << 20),
        cost_estimate=pl.CostEstimate(
            flops=6 * depth * lanes * width * width,
            bytes_accessed=2 * depth * lanes * width,
            transcendentals=0,
        ),
        name="interior",
    )(planes, material, occupancy, moduli, weights)

    share = pl.pallas_call(
        lambda *refs: edge_kernel(rows_y, rows_x, scale, *refs),
        in_specs=[vmem, vmem, vmem, smem, vmem, vmem, vmem],
        out_specs=vmem,
        out_shape=jax.ShapeDtypeStruct((width, width), F32),
        scratch_shapes=[pltpu.VMEM((2, width, lanes), BF16)],
        compiler_params=pltpu.CompilerParams(vmem_limit_bytes=40 << 20),
        cost_estimate=pl.CostEstimate(
            flops=12 * lanes * width * width, bytes_accessed=4 * lanes * width, transcendentals=0
        ),
        name="edge",
    )(top, halo, material, occupancy, moduli, weights, gram)
    return scatter_sum(share, "bricks")


def solution(mesh):
    in_specs = (
        P(("groups", "bricks"), None, None, None),
        P(("groups", "bricks"), None),
        P(("groups", "bricks"), None),
        P(),
    )
    out_specs = P(("groups", "bricks"), None)
    return jax.shard_map(local, mesh=mesh, in_specs=in_specs, out_specs=out_specs, check_vma=False)
```

```python
import jax
import jax.numpy as jnp
import numpy as np
from jax import lax
from jax.experimental import pallas as pl
from jax.experimental.pallas import tpu as pltpu
from jax.sharding import PartitionSpec as P

BLOCK = 256
EDGE = 128
F32 = jnp.float32
BF16 = jnp.bfloat16


def plane_weights(rows_x):
    source = np.arange(BLOCK + 2 * EDGE) - EDGE
    target = np.arange(BLOCK)
    step_y = np.abs(source[:, None] // rows_x - target[None, :] // rows_x)
    step_x = np.abs(source[:, None] % rows_x - target[None, :] % rows_x)
    weight = np.where(step_y == 0, 1.0, 0.5) * np.where(step_x == 0, 1.0, 0.5)
    weight = np.where((step_y <= 1) & (step_x <= 1), weight, 0.0)
    return jnp.asarray(0.5 * weight, BF16)


def lane_place(shape, rows_x):
    lane = lax.broadcasted_iota(jnp.int32, shape, 1)
    return lane // rows_x, lane % rows_x


def brick_select(occupied, rows_y, rows_x, place_y, place_x):
    o = [occupied(t).astype(F32) for t in range(4)]
    low = jnp.where(place_x < rows_x // 2, o[0], o[1])
    high = jnp.where(place_x < rows_x // 2, o[2], o[3])
    return jnp.where(place_y < rows_y // 2, low, high)


def look_up(material, moduli):
    value = jnp.zeros(material.shape, F32)
    for index in range(moduli.shape[1]):
        value = jnp.where(material == index, moduli[:, index : index + 1], value)
    return value


def smooth_plane(value, rows_y, rows_x):
    place_y, place_x = lane_place(value.shape, rows_x)
    lanes = value.shape[1]
    before = jnp.where(place_x > 0, pltpu.roll(value, 1, 1), 0.0)
    after = jnp.where(place_x < rows_x - 1, pltpu.roll(value, lanes - 1, 1), 0.0)
    value = value + 0.5 * (before + after)
    before = jnp.where(place_y > 0, pltpu.roll(value, rows_x, 1), 0.0)
    after = jnp.where(place_y < rows_y - 1, pltpu.roll(value, lanes - rows_x, 1), 0.0)
    return value + 0.5 * (before + after)


def windows(lanes):
    spans = []
    for start in range(0, lanes, BLOCK):
        low = max(start - EDGE, 0)
        high = min(start + BLOCK + EDGE, lanes)
        spans.append((start, low, high))
    return spans


def pack_kernel(
    rows_y, rows_x,
    snapshots_ref, material_hbm, occupied_hbm, moduli_hbm,
    out_ref,
    material_ref, occupied_ref, moduli_ref, plane_ref, rows, sems,
):
    lanes, width = snapshots_ref.shape[1:]
    copies = [
        pltpu.make_async_copy(source, target, sems.at[number])
        for number, (source, target) in enumerate((
            (material_hbm.at[pl.ds(0, 8)], material_ref),
            (occupied_hbm, occupied_ref),
            (moduli_hbm, moduli_ref),
            (snapshots_ref.at[0], plane_ref.at[pl.ds(0, lanes)]),
        ))
    ]
    for copy in copies:
        copy.start()
    for copy in copies[:3]:
        copy.wait()
    occupied = lambda t: occupied_ref[0, t]
    place_y, place_x = lane_place((8, lanes), rows_x)
    value = look_up(material_ref[...], moduli_ref[...].astype(F32))
    value = value * brick_select(occupied, rows_y, rows_x, place_y, place_x)
    rows[...] = jnp.zeros_like(rows)
    for part in range(lanes // width):
        rows[part : part + 1, :] = value[0:1, part * width : (part + 1) * width]
    plane_ref[lanes : lanes + 16, :] = rows[...].astype(BF16)
    copies[3].wait()
    send = pltpu.make_async_copy(plane_ref, out_ref, sems.at[4])
    send.start()
    send.wait()


def main_kernel(
    rows_y, rows_x,
    snapshots_ref, material_ref, occupied_ref, moduli_ref, weights_ref,
    out_ref, top_ref,
    field, field_t, lhs, last, pair, image, modulus_rows, center_columns, masked, sems, top_sem,
):
    depth, lanes, width = snapshots_ref.shape
    blocks = lanes // BLOCK
    per_block = BLOCK // rows_x
    reach = BLOCK + 2 * rows_x
    occupied = lambda t: occupied_ref[0, t]

    def copy(z):
        return pltpu.make_async_copy(snapshots_ref.at[z], field.at[z], sems.at[z])

    for z in range(depth):
        copy(z).start()

    shape = (depth, lanes)
    place_y, place_x = lane_place(shape, rows_x)
    mask = brick_select(occupied, rows_y, rows_x, place_y, place_x)
    modulus = look_up(material_ref[...], moduli_ref[...].astype(F32)) * mask
    smooth = smooth_plane(modulus, rows_y, rows_x)
    place_z = lax.broadcasted_iota(jnp.int32, shape, 0)
    before = jnp.where(place_z > 0, pltpu.roll(smooth, 1, 0), 0.0)
    after = jnp.where(place_z < depth - 1, pltpu.roll(smooth, depth - 1, 0), 0.0)
    smooth = smooth + 0.5 * (before + after)
    center = (4.0 * modulus + 0.5 * smooth) * mask
    for z in range(depth):
        modulus_rows[z] = jnp.broadcast_to(modulus[z : z + 1], (16, lanes)).astype(BF16)
    center_columns[...] = jnp.concatenate([center, jnp.zeros((128 - depth, lanes), F32)], 0).T
    lhs[...] = jnp.zeros_like(lhs)
    on = [occupied(t) > 0 for t in range(4)]
    for block in range(blocks):
        for row in range(0, reach, 16):
            voxel = min(max(block * BLOCK - rows_x + row, 0), lanes - 16)
            brick = voxel // rows_x // (rows_y // 2) * 2 + voxel % rows_x // (rows_x // 2)
            part = weights_ref[EDGE - rows_x + row : EDGE - rows_x + row + 16, :]
            masked[block, row : row + 16, :] = jnp.where(on[brick], part, jnp.zeros_like(part))
    out_ref[...] = jnp.zeros_like(out_ref)

    half = BLOCK // 2
    span = half + 2 * rows_x

    def smoothed(z, block):
        slot = (z * blocks + block) % 2
        scale = modulus_rows[z, :, block * BLOCK : (block + 1) * BLOCK]
        for side in range(2):
            rows = slice(side * (reach - span), side * (reach - span) + span)
            columns = slice(side * half, (side + 1) * half)
            part = masked[block, rows, columns].reshape(span // 16, 16, half)
            lhs[slot, rows, columns] = (part * scale[None, :, columns]).reshape(span, half)
        return jnp.dot(
            lhs[slot], field[z, block * BLOCK : (block + 1) * BLOCK, :],
            preferred_element_type=F32,
        )

    def plane(z, sink):
        above, below = None, None
        for block in range(blocks):
            value = smoothed(z, block)
            own = [value[rows_x * (i + 1) : rows_x * (i + 2)] for i in range(per_block)]
            if block > 0:
                sink(z, per_block * block - 1, above + value[:rows_x])
                own[0] = own[0] + below
            for i in range(per_block - 1):
                sink(z, per_block * block + i, own[i])
            above, below = own[-1], value[rows_x * (per_block + 1) :]
        sink(z, per_block * blocks - 1, above)

    def start(z, y, new):
        last[pl.ds(y * rows_x, rows_x), :] = new

    def write_image(z, rows, both):
        scale = jnp.broadcast_to(center_columns[rows, z : z + 1], (rows_x, width))
        image[z % 2, rows, :] = (scale * field[z, rows, :].astype(F32) - both).astype(BF16)

    def emit(z, y, new):
        rows = pl.ds(y * rows_x, rows_x)
        old = last[rows, :]
        now = old + new
        write_image(z - 1, rows, (old if z == 1 else pair[rows, :]) + now)
        if z == depth - 1:
            write_image(z, rows, now + new)
        else:
            last[rows, :] = new
            pair[rows, :] = now

    def turn(z):
        field_t[z % 2] = field[z].T

    def gram(z):
        out_ref[...] += jnp.dot(field_t[z % 2], image[z % 2], preferred_element_type=F32)

    top = pltpu.make_async_copy(field.at[depth - 1], top_ref, top_sem)
    for z in range(depth):
        if z == 0 or z % 5 == 2:
            for ahead in range(z, min(z + 5 if z else 2, depth)):
                copy(ahead).wait()
                if ahead == depth - 1:
                    top.start()
        if z == 0:
            plane(z, start)
            continue
        if z >= 2:
            gram(z - 2)
        turn(z - 1)
        plane(z, emit)
    gram(depth - 2)
    turn(depth - 1)
    gram(depth - 1)
    top.wait()


def image_block(ft, smooth, m8, c8):
    rows, lanes = ft.shape
    shape = (rows // 8, 8, lanes)
    field = ft.astype(F32).reshape(shape)
    out = c8[None] * field - m8[None] * smooth.reshape(shape)
    return out.reshape(rows, lanes).astype(BF16)


def edge_kernel(
    rows_y, rows_x, scale,
    own, halo_ref, material_ref, occupied_ref, moduli_ref, weights_ref, gram_ref,
    out_ref,
    image,
):
    lanes, width = own.shape
    depth = material_ref.shape[0]
    occupied = lambda t: occupied_ref[0, t]
    shape = (8, lanes)
    place_y, place_x = lane_place(shape, rows_x)
    own_mask = brick_select(occupied, rows_y, rows_x, place_y, place_x)
    value = look_up(material_ref[depth - 8 :, :], moduli_ref[...].astype(F32))
    own_mod = jnp.broadcast_to(value[7:8], shape) * own_mask
    extra = halo_ref[lanes : lanes + 16, :].astype(F32)
    parts = [extra[part : part + 1, :] for part in range(lanes // width)]
    halo_mod = jnp.broadcast_to(jnp.concatenate(parts, axis=1), shape)
    halo_mask = jnp.where(halo_mod > 0.0, 1.0, 0.0)
    own_c = 0.25 * smooth_plane(halo_mod, rows_y, rows_x) * own_mask
    halo_c = 0.25 * smooth_plane(own_mod, rows_y, rows_x) * halo_mask
    halo_t = halo_ref[:lanes, :].T
    halo_on = halo_t * halo_mask[0:1].astype(BF16)
    own_t = own[...].T
    own_on = own_t * own_mask[0:1].astype(BF16)
    for start, low, high in windows(lanes):
        block = slice(start, start + BLOCK)
        first = low - (start - EDGE)
        part = weights_ref[first : first + high - low, :]
        from_halo = jnp.dot(halo_on[:, low:high], part, preferred_element_type=F32)
        from_own = jnp.dot(own_on[:, low:high], part, preferred_element_type=F32)
        image[0, :, block] = image_block(
            own_t[:, block], from_halo, own_mod[:, block], own_c[:, block]
        )
        image[1, :, block] = image_block(
            halo_t[:, block], from_own, halo_mod[:, block], halo_c[:, block]
        )
    total = gram_ref[...]
    total += jnp.dot(image[0], own[...], preferred_element_type=F32)
    total += jnp.dot(image[1], halo_ref[:lanes, :], preferred_element_type=F32)
    out_ref[...] = (total + total.T) * scale


def scatter_sum(value, axis):
    count = lax.axis_size(axis)
    position = lax.axis_index(axis)
    own = value.shape[0] // count
    step = 1
    while step < count:
        value = value.reshape(-1, 2, own, value.shape[-1])
        side = (position // step) % 2
        keep = lax.dynamic_index_in_dim(value, side, 1, keepdims=False)
        give = lax.dynamic_index_in_dim(value, 1 - side, 1, keepdims=False)
        swap = [(device, device ^ step) for device in range(count)]
        value = keep + lax.ppermute(give, axis, swap)
        step *= 2
    return value.reshape(own, value.shape[-1])


def local(snapshots, material, occupancy, moduli):
    depth, rows_y, rows_x, width = snapshots.shape
    lanes = rows_y * rows_x
    owners = lax.axis_size("bricks")
    scale = 1.0 / (depth * lanes * owners)
    planes = snapshots.reshape(depth, lanes, width)
    moduli = moduli.reshape(1, -1)
    weights = plane_weights(rows_x)
    vmem = pl.BlockSpec(memory_space=pltpu.VMEM)
    smem = pl.BlockSpec(memory_space=pltpu.SMEM)
    hbm = pl.BlockSpec(memory_space=pltpu.HBM)
    reach = BLOCK + 2 * rows_x

    packed = pl.pallas_call(
        lambda *refs: pack_kernel(rows_y, rows_x, *refs),
        in_specs=[hbm, hbm, hbm, hbm],
        out_specs=hbm,
        out_shape=jax.ShapeDtypeStruct((lanes + 16, width), BF16),
        scratch_shapes=[
            pltpu.VMEM((8, lanes), material.dtype),
            pltpu.SMEM(occupancy.shape, occupancy.dtype),
            pltpu.VMEM(moduli.shape, moduli.dtype),
            pltpu.VMEM((lanes + 16, width), BF16),
            pltpu.VMEM((16, width), F32),
            pltpu.SemaphoreType.DMA((5,)),
        ],
        compiler_params=pltpu.CompilerParams(vmem_limit_bytes=56 << 20),
        name="pack",
    )(planes, material, occupancy, moduli)

    halo = lax.ppermute(packed, "bricks", [(i + 1, i) for i in range(owners - 1)])

    gram, top = pl.pallas_call(
        lambda *refs: main_kernel(rows_y, rows_x, *refs),
        in_specs=[hbm, vmem, smem, vmem, vmem],
        out_specs=(vmem, hbm),
        out_shape=(
            jax.ShapeDtypeStruct((width, width), F32),
            jax.ShapeDtypeStruct((lanes, width), BF16),
        ),
        scratch_shapes=[
            pltpu.VMEM((depth, lanes, width), BF16),
            pltpu.VMEM((2, width, lanes), BF16),
            pltpu.VMEM((2, reach, BLOCK), BF16),
            pltpu.VMEM((lanes, width), F32),
            pltpu.VMEM((lanes, width), F32),
            pltpu.VMEM((2, lanes, width), BF16),
            pltpu.VMEM((depth, 16, lanes), BF16),
            pltpu.VMEM((lanes, 128), F32),
            pltpu.VMEM((lanes // BLOCK, reach, BLOCK), BF16),
            pltpu.SemaphoreType.DMA((depth,)),
            pltpu.SemaphoreType.DMA(()),
        ],
        compiler_params=pltpu.CompilerParams(vmem_limit_bytes=52 << 20),
        cost_estimate=pl.CostEstimate(
            flops=6 * depth * lanes * width * width,
            bytes_accessed=2 * depth * lanes * width,
            transcendentals=0,
        ),
        name="interior",
    )(planes, material, occupancy, moduli, weights)

    share = pl.pallas_call(
        lambda *refs: edge_kernel(rows_y, rows_x, scale, *refs),
        in_specs=[vmem, vmem, vmem, smem, vmem, vmem, vmem],
        out_specs=vmem,
        out_shape=jax.ShapeDtypeStruct((width, width), F32),
        scratch_shapes=[pltpu.VMEM((2, width, lanes), BF16)],
        compiler_params=pltpu.CompilerParams(vmem_limit_bytes=40 << 20),
        cost_estimate=pl.CostEstimate(
            flops=12 * lanes * width * width, bytes_accessed=4 * lanes * width, transcendentals=0
        ),
        name="edge",
    )(top, halo, material, occupancy, moduli, weights, gram)
    return scatter_sum(share, "bricks")


def solution(mesh):
    in_specs = (
        P(("groups", "bricks"), None, None, None),
        P(("groups", "bricks"), None),
        P(("groups", "bricks"), None),
        P(),
    )
    out_specs = P(("groups", "bricks"), None)
    return jax.shard_map(local, mesh=mesh, in_specs=in_specs, out_specs=out_specs, check_vma=False)
```

```python
import jax
import jax.numpy as jnp
import numpy as np
from jax import lax
from jax.experimental import pallas as pl
from jax.experimental.pallas import tpu as pltpu
from jax.sharding import PartitionSpec as P

BLOCK = 256
EDGE = 128
F32 = jnp.float32
BF16 = jnp.bfloat16


def plane_weights(rows_x):
    source = np.arange(BLOCK + 2 * EDGE) - EDGE
    target = np.arange(BLOCK)
    step_y = np.abs(source[:, None] // rows_x - target[None, :] // rows_x)
    step_x = np.abs(source[:, None] % rows_x - target[None, :] % rows_x)
    weight = np.where(step_y == 0, 1.0, 0.5) * np.where(step_x == 0, 1.0, 0.5)
    weight = np.where((step_y <= 1) & (step_x <= 1), weight, 0.0)
    return jnp.asarray(0.5 * weight, BF16)


def lane_place(shape, rows_x):
    lane = lax.broadcasted_iota(jnp.int32, shape, 1)
    return lane // rows_x, lane % rows_x


def brick_select(occupied, rows_y, rows_x, place_y, place_x):
    o = [occupied(t).astype(F32) for t in range(4)]
    low = jnp.where(place_x < rows_x // 2, o[0], o[1])
    high = jnp.where(place_x < rows_x // 2, o[2], o[3])
    return jnp.where(place_y < rows_y // 2, low, high)


def look_up(material, moduli):
    value = jnp.zeros(material.shape, F32)
    for index in range(moduli.shape[1]):
        value = jnp.where(material == index, moduli[:, index : index + 1], value)
    return value


def smooth_plane(value, rows_y, rows_x):
    place_y, place_x = lane_place(value.shape, rows_x)
    lanes = value.shape[1]
    before = jnp.where(place_x > 0, pltpu.roll(value, 1, 1), 0.0)
    after = jnp.where(place_x < rows_x - 1, pltpu.roll(value, lanes - 1, 1), 0.0)
    value = value + 0.5 * (before + after)
    before = jnp.where(place_y > 0, pltpu.roll(value, rows_x, 1), 0.0)
    after = jnp.where(place_y < rows_y - 1, pltpu.roll(value, lanes - rows_x, 1), 0.0)
    return value + 0.5 * (before + after)


def windows(lanes):
    spans = []
    for start in range(0, lanes, BLOCK):
        low = max(start - EDGE, 0)
        high = min(start + BLOCK + EDGE, lanes)
        spans.append((start, low, high))
    return spans


def pack_kernel(
    rows_y, rows_x,
    snapshots_ref, material_hbm, occupied_hbm, moduli_hbm,
    out_ref,
    material_ref, occupied_ref, moduli_ref, plane_ref, rows, sems,
):
    lanes, width = snapshots_ref.shape[1:]
    parts = 4
    size = lanes // parts
    copies = [
        pltpu.make_async_copy(source, target, sems.at[number])
        for number, (source, target) in enumerate((
            (material_hbm.at[pl.ds(0, 8)], material_ref),
            (occupied_hbm, occupied_ref),
            (moduli_hbm, moduli_ref),
        ))
    ]
    pieces = [pl.ds(part * size, size) for part in range(parts)]
    loads = [
        pltpu.make_async_copy(snapshots_ref.at[0, piece], plane_ref.at[piece], sems.at[3 + number])
        for number, piece in enumerate(pieces)
    ]
    for copy in copies + loads:
        copy.start()
    pieces.append(pl.ds(lanes, 16))
    sends = [
        pltpu.make_async_copy(plane_ref.at[piece], out_ref.at[piece], sems.at[3 + parts + number])
        for number, piece in enumerate(pieces)
    ]
    for load, send in zip(loads, sends):
        load.wait()
        send.start()
    for copy in copies:
        copy.wait()
    occupied = lambda t: occupied_ref[0, t]
    place_y, place_x = lane_place((8, lanes), rows_x)
    value = look_up(material_ref[...], moduli_ref[...].astype(F32))
    value = value * brick_select(occupied, rows_y, rows_x, place_y, place_x)
    rows[...] = jnp.zeros_like(rows)
    for part in range(lanes // width):
        rows[part : part + 1, :] = value[0:1, part * width : (part + 1) * width]
    plane_ref[lanes : lanes + 16, :] = rows[...].astype(BF16)
    sends[-1].start()
    for send in sends:
        send.wait()


def main_kernel(
    rows_y, rows_x,
    snapshots_ref, material_ref, occupied_ref, moduli_ref, weights_ref,
    out_ref, top_ref,
    field, field_t, lhs, last, pair, image, modulus_rows, center_columns, masked, sems, top_sem,
):
    depth, lanes, width = snapshots_ref.shape
    blocks = lanes // BLOCK
    per_block = BLOCK // rows_x
    reach = BLOCK + 2 * rows_x
    occupied = lambda t: occupied_ref[0, t]

    def copy(z):
        return pltpu.make_async_copy(snapshots_ref.at[z], field.at[z], sems.at[z])

    for z in range(depth):
        copy(z).start()

    shape = (depth, lanes)
    place_y, place_x = lane_place(shape, rows_x)
    mask = brick_select(occupied, rows_y, rows_x, place_y, place_x)
    modulus = look_up(material_ref[...], moduli_ref[...].astype(F32)) * mask
    smooth = smooth_plane(modulus, rows_y, rows_x)
    place_z = lax.broadcasted_iota(jnp.int32, shape, 0)
    before = jnp.where(place_z > 0, pltpu.roll(smooth, 1, 0), 0.0)
    after = jnp.where(place_z < depth - 1, pltpu.roll(smooth, depth - 1, 0), 0.0)
    smooth = smooth + 0.5 * (before + after)
    center = (4.0 * modulus + 0.5 * smooth) * mask
    for z in range(depth):
        modulus_rows[z] = jnp.broadcast_to(modulus[z : z + 1], (16, lanes)).astype(BF16)
    center_columns[...] = jnp.concatenate([center, jnp.zeros((128 - depth, lanes), F32)], 0).T
    lhs[...] = jnp.zeros_like(lhs)
    on = [occupied(t) > 0 for t in range(4)]
    for block in range(blocks):
        for row in range(0, reach, 16):
            voxel = min(max(block * BLOCK - rows_x + row, 0), lanes - 16)
            brick = voxel // rows_x // (rows_y // 2) * 2 + voxel % rows_x // (rows_x // 2)
            part = weights_ref[EDGE - rows_x + row : EDGE - rows_x + row + 16, :]
            masked[block, row : row + 16, :] = jnp.where(on[brick], part, jnp.zeros_like(part))
    out_ref[...] = jnp.zeros_like(out_ref)

    half = BLOCK // 2
    span = half + 2 * rows_x

    def smoothed(z, block):
        slot = (z * blocks + block) % 2
        scale = modulus_rows[z, :, block * BLOCK : (block + 1) * BLOCK]
        for side in range(2):
            rows = slice(side * (reach - span), side * (reach - span) + span)
            columns = slice(side * half, (side + 1) * half)
            part = masked[block, rows, columns].reshape(span // 16, 16, half)
            lhs[slot, rows, columns] = (part * scale[None, :, columns]).reshape(span, half)
        return jnp.dot(
            lhs[slot], field[z, block * BLOCK : (block + 1) * BLOCK, :],
            preferred_element_type=F32,
        )

    def plane(z, sink):
        above, below = None, None
        for block in range(blocks):
            value = smoothed(z, block)
            own = [value[rows_x * (i + 1) : rows_x * (i + 2)] for i in range(per_block)]
            if block > 0:
                sink(z, per_block * block - 1, above + value[:rows_x])
                own[0] = own[0] + below
            for i in range(per_block - 1):
                sink(z, per_block * block + i, own[i])
            above, below = own[-1], value[rows_x * (per_block + 1) :]
        sink(z, per_block * blocks - 1, above)

    def start(z, y, new):
        last[pl.ds(y * rows_x, rows_x), :] = new

    def write_image(z, rows, both):
        scale = jnp.broadcast_to(center_columns[rows, z : z + 1], (rows_x, width))
        image[z % 2, rows, :] = (scale * field[z, rows, :].astype(F32) - both).astype(BF16)

    def emit(z, y, new):
        rows = pl.ds(y * rows_x, rows_x)
        old = last[rows, :]
        now = old + new
        write_image(z - 1, rows, (old if z == 1 else pair[rows, :]) + now)
        if z == depth - 1:
            write_image(z, rows, now + new)
        else:
            last[rows, :] = new
            pair[rows, :] = now

    def turn(z):
        field_t[z % 2] = field[z].T

    def gram(z):
        out_ref[...] += jnp.dot(field_t[z % 2], image[z % 2], preferred_element_type=F32)

    top = pltpu.make_async_copy(field.at[depth - 1], top_ref, top_sem)
    for z in range(depth):
        if z == 0 or z % 5 == 2:
            for ahead in range(z, min(z + 5 if z else 2, depth)):
                copy(ahead).wait()
                if ahead == depth - 1:
                    top.start()
        if z == 0:
            plane(z, start)
            continue
        if z >= 2:
            gram(z - 2)
        turn(z - 1)
        plane(z, emit)
    gram(depth - 2)
    turn(depth - 1)
    gram(depth - 1)
    top.wait()


def image_block(ft, smooth, m8, c8):
    rows, lanes = ft.shape
    shape = (rows // 8, 8, lanes)
    field = ft.astype(F32).reshape(shape)
    out = c8[None] * field - m8[None] * smooth.reshape(shape)
    return out.reshape(rows, lanes).astype(BF16)


def edge_kernel(
    rows_y, rows_x, scale,
    own, halo_ref, material_ref, occupied_ref, moduli_ref, weights_ref, gram_ref,
    out_ref,
    image,
):
    lanes, width = own.shape
    depth = material_ref.shape[0]
    occupied = lambda t: occupied_ref[0, t]
    shape = (8, lanes)
    place_y, place_x = lane_place(shape, rows_x)
    own_mask = brick_select(occupied, rows_y, rows_x, place_y, place_x)
    value = look_up(material_ref[depth - 8 :, :], moduli_ref[...].astype(F32))
    own_mod = jnp.broadcast_to(value[7:8], shape) * own_mask
    extra = halo_ref[lanes : lanes + 16, :].astype(F32)
    parts = [extra[part : part + 1, :] for part in range(lanes // width)]
    halo_mod = jnp.broadcast_to(jnp.concatenate(parts, axis=1), shape)
    halo_mask = jnp.where(halo_mod > 0.0, 1.0, 0.0)
    own_c = 0.25 * smooth_plane(halo_mod, rows_y, rows_x) * own_mask
    halo_c = 0.25 * smooth_plane(own_mod, rows_y, rows_x) * halo_mask
    halo_t = halo_ref[:lanes, :].T
    halo_on = halo_t * halo_mask[0:1].astype(BF16)
    own_t = own[...].T
    own_on = own_t * own_mask[0:1].astype(BF16)
    for start, low, high in windows(lanes):
        block = slice(start, start + BLOCK)
        first = low - (start - EDGE)
        part = weights_ref[first : first + high - low, :]
        from_halo = jnp.dot(halo_on[:, low:high], part, preferred_element_type=F32)
        from_own = jnp.dot(own_on[:, low:high], part, preferred_element_type=F32)
        image[0, :, block] = image_block(
            own_t[:, block], from_halo, own_mod[:, block], own_c[:, block]
        )
        image[1, :, block] = image_block(
            halo_t[:, block], from_own, halo_mod[:, block], halo_c[:, block]
        )
    total = gram_ref[...]
    total += jnp.dot(image[0], own[...], preferred_element_type=F32)
    total += jnp.dot(image[1], halo_ref[:lanes, :], preferred_element_type=F32)
    out_ref[...] = (total + total.T) * scale


def scatter_sum(value, axis):
    count = lax.axis_size(axis)
    position = lax.axis_index(axis)
    own = value.shape[0] // count
    step = 1
    while step < count:
        value = value.reshape(-1, 2, own, value.shape[-1])
        side = (position // step) % 2
        keep = lax.dynamic_index_in_dim(value, side, 1, keepdims=False)
        give = lax.dynamic_index_in_dim(value, 1 - side, 1, keepdims=False)
        swap = [(device, device ^ step) for device in range(count)]
        value = keep + lax.ppermute(give, axis, swap)
        step *= 2
    return value.reshape(own, value.shape[-1])


def local(snapshots, material, occupancy, moduli):
    depth, rows_y, rows_x, width = snapshots.shape
    lanes = rows_y * rows_x
    owners = lax.axis_size("bricks")
    scale = 1.0 / (depth * lanes * owners)
    planes = snapshots.reshape(depth, lanes, width)
    moduli = moduli.reshape(1, -1)
    weights = plane_weights(rows_x)
    vmem = pl.BlockSpec(memory_space=pltpu.VMEM)
    smem = pl.BlockSpec(memory_space=pltpu.SMEM)
    hbm = pl.BlockSpec(memory_space=pltpu.HBM)
    reach = BLOCK + 2 * rows_x

    packed = pl.pallas_call(
        lambda *refs: pack_kernel(rows_y, rows_x, *refs),
        in_specs=[hbm, hbm, hbm, hbm],
        out_specs=hbm,
        out_shape=jax.ShapeDtypeStruct((lanes + 16, width), BF16),
        scratch_shapes=[
            pltpu.VMEM((8, lanes), material.dtype),
            pltpu.SMEM(occupancy.shape, occupancy.dtype),
            pltpu.VMEM(moduli.shape, moduli.dtype),
            pltpu.VMEM((lanes + 16, width), BF16),
            pltpu.VMEM((16, width), F32),
            pltpu.SemaphoreType.DMA((12,)),
        ],
        compiler_params=pltpu.CompilerParams(vmem_limit_bytes=56 << 20),
        name="pack",
    )(planes, material, occupancy, moduli)

    halo = lax.ppermute(packed, "bricks", [(i + 1, i) for i in range(owners - 1)])

    gram, top = pl.pallas_call(
        lambda *refs: main_kernel(rows_y, rows_x, *refs),
        in_specs=[hbm, vmem, smem, vmem, vmem],
        out_specs=(vmem, hbm),
        out_shape=(
            jax.ShapeDtypeStruct((width, width), F32),
            jax.ShapeDtypeStruct((lanes, width), BF16),
        ),
        scratch_shapes=[
            pltpu.VMEM((depth, lanes, width), BF16),
            pltpu.VMEM((2, width, lanes), BF16),
            pltpu.VMEM((2, reach, BLOCK), BF16),
            pltpu.VMEM((lanes, width), F32),
            pltpu.VMEM((lanes, width), F32),
            pltpu.VMEM((2, lanes, width), BF16),
            pltpu.VMEM((depth, 16, lanes), BF16),
            pltpu.VMEM((lanes, 128), F32),
            pltpu.VMEM((lanes // BLOCK, reach, BLOCK), BF16),
            pltpu.SemaphoreType.DMA((depth,)),
            pltpu.SemaphoreType.DMA(()),
        ],
        compiler_params=pltpu.CompilerParams(vmem_limit_bytes=52 << 20),
        cost_estimate=pl.CostEstimate(
            flops=6 * depth * lanes * width * width,
            bytes_accessed=2 * depth * lanes * width,
            transcendentals=0,
        ),
        name="interior",
    )(planes, material, occupancy, moduli, weights)

    share = pl.pallas_call(
        lambda *refs: edge_kernel(rows_y, rows_x, scale, *refs),
        in_specs=[vmem, vmem, vmem, smem, vmem, vmem, vmem],
        out_specs=vmem,
        out_shape=jax.ShapeDtypeStruct((width, width), F32),
        scratch_shapes=[pltpu.VMEM((2, width, lanes), BF16)],
        compiler_params=pltpu.CompilerParams(vmem_limit_bytes=40 << 20),
        cost_estimate=pl.CostEstimate(
            flops=12 * lanes * width * width, bytes_accessed=4 * lanes * width, transcendentals=0
        ),
        name="edge",
    )(top, halo, material, occupancy, moduli, weights, gram)
    return scatter_sum(share, "bricks")


def solution(mesh):
    in_specs = (
        P(("groups", "bricks"), None, None, None),
        P(("groups", "bricks"), None),
        P(("groups", "bricks"), None),
        P(),
    )
    out_specs = P(("groups", "bricks"), None)
    return jax.shard_map(local, mesh=mesh, in_specs=in_specs, out_specs=out_specs, check_vma=False)
```

```python
import jax
import jax.numpy as jnp
import numpy as np
from jax import lax
from jax.experimental import pallas as pl
from jax.experimental.pallas import tpu as pltpu
from jax.sharding import PartitionSpec as P

BLOCK = 256
EDGE = 128
F32 = jnp.float32
BF16 = jnp.bfloat16


def plane_weights(rows_x):
    source = np.arange(BLOCK + 2 * EDGE) - EDGE
    target = np.arange(BLOCK)
    step_y = np.abs(source[:, None] // rows_x - target[None, :] // rows_x)
    step_x = np.abs(source[:, None] % rows_x - target[None, :] % rows_x)
    weight = np.where(step_y == 0, 1.0, 0.5) * np.where(step_x == 0, 1.0, 0.5)
    weight = np.where((step_y <= 1) & (step_x <= 1), weight, 0.0)
    return jnp.asarray(0.5 * weight, BF16)


def lane_place(shape, rows_x):
    lane = lax.broadcasted_iota(jnp.int32, shape, 1)
    return lane // rows_x, lane % rows_x


def brick_select(occupied, rows_y, rows_x, place_y, place_x):
    o = [occupied(t).astype(F32) for t in range(4)]
    low = jnp.where(place_x < rows_x // 2, o[0], o[1])
    high = jnp.where(place_x < rows_x // 2, o[2], o[3])
    return jnp.where(place_y < rows_y // 2, low, high)


def look_up(material, moduli):
    value = jnp.zeros(material.shape, F32)
    for index in range(moduli.shape[1]):
        value = jnp.where(material == index, moduli[:, index : index + 1], value)
    return value


def smooth_plane(value, rows_y, rows_x):
    place_y, place_x = lane_place(value.shape, rows_x)
    lanes = value.shape[1]
    before = jnp.where(place_x > 0, pltpu.roll(value, 1, 1), 0.0)
    after = jnp.where(place_x < rows_x - 1, pltpu.roll(value, lanes - 1, 1), 0.0)
    value = value + 0.5 * (before + after)
    before = jnp.where(place_y > 0, pltpu.roll(value, rows_x, 1), 0.0)
    after = jnp.where(place_y < rows_y - 1, pltpu.roll(value, lanes - rows_x, 1), 0.0)
    return value + 0.5 * (before + after)


def windows(lanes):
    spans = []
    for start in range(0, lanes, BLOCK):
        low = max(start - EDGE, 0)
        high = min(start + BLOCK + EDGE, lanes)
        spans.append((start, low, high))
    return spans


def pack_kernel(
    rows_y, rows_x,
    snapshots_ref, material_hbm, occupied_hbm, moduli_hbm,
    out_ref,
    material_ref, occupied_ref, moduli_ref, plane_ref, rows, sems,
):
    lanes, width = snapshots_ref.shape[1:]
    copies = [
        pltpu.make_async_copy(source, target, sems.at[number])
        for number, (source, target) in enumerate((
            (material_hbm.at[pl.ds(0, 8)], material_ref),
            (occupied_hbm, occupied_ref),
            (moduli_hbm, moduli_ref),
            (snapshots_ref.at[0], plane_ref.at[pl.ds(0, lanes)]),
        ))
    ]
    for copy in copies:
        copy.start()
    for copy in copies[:3]:
        copy.wait()
    occupied = lambda t: occupied_ref[0, t]
    place_y, place_x = lane_place((8, lanes), rows_x)
    value = look_up(material_ref[...], moduli_ref[...].astype(F32))
    value = value * brick_select(occupied, rows_y, rows_x, place_y, place_x)
    rows[...] = jnp.zeros_like(rows)
    for part in range(lanes // width):
        rows[part : part + 1, :] = value[0:1, part * width : (part + 1) * width]
    plane_ref[lanes : lanes + 16, :] = rows[...].astype(BF16)
    copies[3].wait()
    send = pltpu.make_async_copy(plane_ref, out_ref, sems.at[4])
    send.start()
    send.wait()


def main_kernel(
    rows_y, rows_x,
    snapshots_ref, material_ref, occupied_ref, moduli_ref, weights_ref,
    out_ref, top_ref,
    field, field_t, lhs, last, pair, image, modulus_rows, center_columns, masked, sems, top_sem,
):
    depth, lanes, width = snapshots_ref.shape
    blocks = lanes // BLOCK
    per_block = BLOCK // rows_x
    reach = BLOCK + 2 * rows_x
    occupied = lambda t: occupied_ref[0, t]

    def copy(z):
        return pltpu.make_async_copy(snapshots_ref.at[z], field.at[z], sems.at[z])

    for z in range(depth):
        copy(z).start()

    shape = (depth, lanes)
    place_y, place_x = lane_place(shape, rows_x)
    mask = brick_select(occupied, rows_y, rows_x, place_y, place_x)
    modulus = look_up(material_ref[...], moduli_ref[...].astype(F32)) * mask
    smooth = smooth_plane(modulus, rows_y, rows_x)
    place_z = lax.broadcasted_iota(jnp.int32, shape, 0)
    before = jnp.where(place_z > 0, pltpu.roll(smooth, 1, 0), 0.0)
    after = jnp.where(place_z < depth - 1, pltpu.roll(smooth, depth - 1, 0), 0.0)
    smooth = smooth + 0.5 * (before + after)
    center = (4.0 * modulus + 0.5 * smooth) * mask
    for z in range(depth):
        modulus_rows[z] = jnp.broadcast_to(modulus[z : z + 1], (16, lanes)).astype(BF16)
    center_columns[...] = jnp.concatenate([center, jnp.zeros((128 - depth, lanes), F32)], 0).T
    lhs[...] = jnp.zeros_like(lhs)
    on = [occupied(t) > 0 for t in range(4)]
    for block in range(blocks):
        for row in range(0, reach, 16):
            voxel = min(max(block * BLOCK - rows_x + row, 0), lanes - 16)
            brick = voxel // rows_x // (rows_y // 2) * 2 + voxel % rows_x // (rows_x // 2)
            part = weights_ref[EDGE - rows_x + row : EDGE - rows_x + row + 16, :]
            masked[block, row : row + 16, :] = jnp.where(on[brick], part, jnp.zeros_like(part))
    out_ref[...] = jnp.zeros_like(out_ref)

    half = BLOCK // 2
    span = half + 2 * rows_x

    def smoothed(z, block):
        slot = (z * blocks + block) % 2
        scale = modulus_rows[z, :, block * BLOCK : (block + 1) * BLOCK]
        for side in range(2):
            rows = slice(side * (reach - span), side * (reach - span) + span)
            columns = slice(side * half, (side + 1) * half)
            part = masked[block, rows, columns].reshape(span // 16, 16, half)
            lhs[slot, rows, columns] = (part * scale[None, :, columns]).reshape(span, half)
        return jnp.dot(
            lhs[slot], field[z, block * BLOCK : (block + 1) * BLOCK, :],
            preferred_element_type=F32,
        )

    def plane(z, sink):
        above, below = None, None
        for block in range(blocks):
            value = smoothed(z, block)
            own = [value[rows_x * (i + 1) : rows_x * (i + 2)] for i in range(per_block)]
            if block > 0:
                sink(z, per_block * block - 1, above + value[:rows_x])
                own[0] = own[0] + below
            for i in range(per_block - 1):
                sink(z, per_block * block + i, own[i])
            above, below = own[-1], value[rows_x * (per_block + 1) :]
        sink(z, per_block * blocks - 1, above)

    def start(z, y, new):
        last[pl.ds(y * rows_x, rows_x), :] = new

    def write_image(z, rows, both):
        scale = jnp.broadcast_to(center_columns[rows, z : z + 1], (rows_x, width))
        image[z % 2, rows, :] = (scale * field[z, rows, :].astype(F32) - both).astype(BF16)

    def emit(z, y, new):
        rows = pl.ds(y * rows_x, rows_x)
        old = last[rows, :]
        now = old + new
        write_image(z - 1, rows, (old if z == 1 else pair[rows, :]) + now)
        if z == depth - 1:
            write_image(z, rows, now + new)
        else:
            last[rows, :] = new
            pair[rows, :] = now

    def turn(z):
        field_t[z % 2] = field[z].T

    def gram(z):
        out_ref[...] += jnp.dot(field_t[z % 2], image[z % 2], preferred_element_type=F32)

    top = pltpu.make_async_copy(field.at[depth - 1], top_ref, top_sem)
    for z in range(depth):
        if z == 0 or z % 5 == 2:
            for ahead in range(z, min(z + 5 if z else 2, depth)):
                copy(ahead).wait()
                if ahead == depth - 1:
                    top.start()
        if z == 0:
            plane(z, start)
            continue
        if z >= 2:
            gram(z - 2)
        turn(z - 1)
        plane(z, emit)
    gram(depth - 2)
    turn(depth - 1)
    gram(depth - 1)
    top.wait()


def image_block(ft, smooth, m8, c8):
    rows, lanes = ft.shape
    shape = (rows // 8, 8, lanes)
    field = ft.astype(F32).reshape(shape)
    out = c8[None] * field - m8[None] * smooth.reshape(shape)
    return out.reshape(rows, lanes).astype(BF16)


def edge_kernel(
    rows_y, rows_x, scale,
    own, halo_ref, material_ref, occupied_ref, moduli_ref, weights_ref, gram_ref,
    out_ref,
    image, turned, kept,
):
    lanes, width = own.shape
    depth = material_ref.shape[0]
    occupied = lambda t: occupied_ref[0, t]
    shape = (8, lanes)
    place_y, place_x = lane_place(shape, rows_x)
    own_mask = brick_select(occupied, rows_y, rows_x, place_y, place_x)
    value = look_up(material_ref[depth - 8 :, :], moduli_ref[...].astype(F32))
    own_mod = jnp.broadcast_to(value[7:8], shape) * own_mask
    extra = halo_ref[lanes : lanes + 16, :].astype(F32)
    parts = [extra[part : part + 1, :] for part in range(lanes // width)]
    halo_mod = jnp.broadcast_to(jnp.concatenate(parts, axis=1), shape)
    halo_mask = jnp.where(halo_mod > 0.0, 1.0, 0.0)
    own_c = 0.25 * smooth_plane(halo_mod, rows_y, rows_x) * own_mask
    halo_c = 0.25 * smooth_plane(own_mod, rows_y, rows_x) * halo_mask
    turned[0] = halo_ref[:lanes, :].T
    turned[1] = own[...].T
    kept[0] = turned[0] * halo_mask[0:1].astype(BF16)
    kept[1] = turned[1] * own_mask[0:1].astype(BF16)
    for start, low, high in windows(lanes):
        block = slice(start, start + BLOCK)
        first = low - (start - EDGE)
        part = weights_ref[first : first + high - low, :]
        from_halo = jnp.dot(kept[0, :, low:high], part, preferred_element_type=F32)
        image[0, :, block] = image_block(
            turned[1, :, block], from_halo, own_mod[:, block], own_c[:, block]
        )
        from_own = jnp.dot(kept[1, :, low:high], part, preferred_element_type=F32)
        image[1, :, block] = image_block(
            turned[0, :, block], from_own, halo_mod[:, block], halo_c[:, block]
        )
    total = gram_ref[...]
    total += jnp.dot(image[0], own[...], preferred_element_type=F32)
    total += jnp.dot(image[1], halo_ref[:lanes, :], preferred_element_type=F32)
    out_ref[...] = (total + total.T) * scale


def scatter_sum(value, axis):
    count = lax.axis_size(axis)
    position = lax.axis_index(axis)
    own = value.shape[0] // count
    step = 1
    while step < count:
        value = value.reshape(-1, 2, own, value.shape[-1])
        side = (position // step) % 2
        keep = lax.dynamic_index_in_dim(value, side, 1, keepdims=False)
        give = lax.dynamic_index_in_dim(value, 1 - side, 1, keepdims=False)
        swap = [(device, device ^ step) for device in range(count)]
        value = keep + lax.ppermute(give, axis, swap)
        step *= 2
    return value.reshape(own, value.shape[-1])


def local(snapshots, material, occupancy, moduli):
    depth, rows_y, rows_x, width = snapshots.shape
    lanes = rows_y * rows_x
    owners = lax.axis_size("bricks")
    scale = 1.0 / (depth * lanes * owners)
    planes = snapshots.reshape(depth, lanes, width)
    moduli = moduli.reshape(1, -1)
    weights = plane_weights(rows_x)
    vmem = pl.BlockSpec(memory_space=pltpu.VMEM)
    smem = pl.BlockSpec(memory_space=pltpu.SMEM)
    hbm = pl.BlockSpec(memory_space=pltpu.HBM)
    reach = BLOCK + 2 * rows_x

    packed = pl.pallas_call(
        lambda *refs: pack_kernel(rows_y, rows_x, *refs),
        in_specs=[hbm, hbm, hbm, hbm],
        out_specs=hbm,
        out_shape=jax.ShapeDtypeStruct((lanes + 16, width), BF16),
        scratch_shapes=[
            pltpu.VMEM((8, lanes), material.dtype),
            pltpu.SMEM(occupancy.shape, occupancy.dtype),
            pltpu.VMEM(moduli.shape, moduli.dtype),
            pltpu.VMEM((lanes + 16, width), BF16),
            pltpu.VMEM((16, width), F32),
            pltpu.SemaphoreType.DMA((5,)),
        ],
        compiler_params=pltpu.CompilerParams(vmem_limit_bytes=56 << 20),
        name="pack",
    )(planes, material, occupancy, moduli)

    halo = lax.ppermute(packed, "bricks", [(i + 1, i) for i in range(owners - 1)])

    gram, top = pl.pallas_call(
        lambda *refs: main_kernel(rows_y, rows_x, *refs),
        in_specs=[hbm, vmem, smem, vmem, vmem],
        out_specs=(vmem, hbm),
        out_shape=(
            jax.ShapeDtypeStruct((width, width), F32),
            jax.ShapeDtypeStruct((lanes, width), BF16),
        ),
        scratch_shapes=[
            pltpu.VMEM((depth, lanes, width), BF16),
            pltpu.VMEM((2, width, lanes), BF16),
            pltpu.VMEM((2, reach, BLOCK), BF16),
            pltpu.VMEM((lanes, width), F32),
            pltpu.VMEM((lanes, width), F32),
            pltpu.VMEM((2, lanes, width), BF16),
            pltpu.VMEM((depth, 16, lanes), BF16),
            pltpu.VMEM((lanes, 128), F32),
            pltpu.VMEM((lanes // BLOCK, reach, BLOCK), BF16),
            pltpu.SemaphoreType.DMA((depth,)),
            pltpu.SemaphoreType.DMA(()),
        ],
        compiler_params=pltpu.CompilerParams(vmem_limit_bytes=52 << 20),
        cost_estimate=pl.CostEstimate(
            flops=6 * depth * lanes * width * width,
            bytes_accessed=2 * depth * lanes * width,
            transcendentals=0,
        ),
        name="interior",
    )(planes, material, occupancy, moduli, weights)

    share = pl.pallas_call(
        lambda *refs: edge_kernel(rows_y, rows_x, scale, *refs),
        in_specs=[vmem, vmem, vmem, smem, vmem, vmem, vmem],
        out_specs=vmem,
        out_shape=jax.ShapeDtypeStruct((width, width), F32),
        scratch_shapes=[pltpu.VMEM((2, width, lanes), BF16)] * 3,
        compiler_params=pltpu.CompilerParams(vmem_limit_bytes=40 << 20),
        cost_estimate=pl.CostEstimate(
            flops=12 * lanes * width * width, bytes_accessed=4 * lanes * width, transcendentals=0
        ),
        name="edge",
    )(top, halo, material, occupancy, moduli, weights, gram)
    return scatter_sum(share, "bricks")


def solution(mesh):
    in_specs = (
        P(("groups", "bricks"), None, None, None),
        P(("groups", "bricks"), None),
        P(("groups", "bricks"), None),
        P(),
    )
    out_specs = P(("groups", "bricks"), None)
    return jax.shard_map(local, mesh=mesh, in_specs=in_specs, out_specs=out_specs, check_vma=False)
```
